256 devices in a mesh: tok: 32 (over z, x), hid: 8 (over y, core).
Axes of the slice: x: 4, y: 4, z: 8, core: 2. Of those that a mesh axis runs over, the one named last changes fastest.
Arguments:
- inputs: float32 [4096, 4096], P('tok'), may hold values from -6 to 6
- cotangent: float32 [4096, 4096], P('tok'), may hold values from -6 to 6
- up_blocks: float32 [112, 4, 128, 128], P('hid', None, 'tok'), may hold values from -0.25 to 0.25
- down_blocks: float32 [112, 4, 128, 128], P('hid', None, 'tok'), may hold values from -0.25 to 0.25
- up_index: int32 [112, 4], P('hid'), may hold values from 0 to 31, all different within a row
- down_index: int32 [112, 4], P('hid'), may hold values from 0 to 31, all different within a row
- mom_up: float32 [112, 4, 128, 128], P('hid', None, 'tok'), may hold values from -6 to 6
- mom_down: float32 [112, 4, 128, 128], P('hid', None, 'tok'), may hold values from -6 to 6
Outputs:
- input_grad: float32 [4096, 4096], P('tok', 'hid')
- new_mom_up: float32 [112, 4, 128, 128], P('hid', None, 'tok')
- new_mom_down: float32 [112, 4, 128, 128], P('hid', None, 'tok')
The draws below stay inside these ranges and needn't reach their ends.
Inputs may be any that keep to these rules, and one draw needn't show every extreme that they name: `up_index`: each row lists 4 different model blocks, and every model block appears in some row. `down_index`: each row lists 4 different model blocks, and every model block appears in some row.
All inputs are finite; a program needn't handle non-finite values.
Results may differ from the reference program's by a relative error of at most 0.0003.
Values sent between devices are 32-bit elements; how exact they have to be, the bound alone decides.
A program may use at most 64 MiB of HBM per device.

```python
import jax
import jax.numpy as jnp
from jax import lax

D = 4096
BLK = 128
KB = 4
TOKENS = 4096
FFB = 112


def shard_levels(own_key, extent, pieces, low, largest):
    def one(position, parts):
        heights = jax.random.uniform(jax.random.fold_in(jax.random.fold_in(own_key, 6), position), (parts,), jnp.float32, low / len(pieces), largest / len(pieces))
        return jnp.repeat(jnp.exp(heights), extent[position] // parts).reshape((-1,) + (1,) * (len(extent) - position - 1))

    level = one(*pieces[0])
    for cut in pieces[1:]:
        level = level * one(*cut)
    return level


def picks_of(rng, rows, count, top, lift):
    ranking = jax.random.permutation(jax.random.fold_in(rng, 1), count)
    boost = ranking
    for power in range(3):
        boost = boost * boost // count
    boost = boost * lift // count
    chance = jax.random.randint(jax.random.fold_in(rng, 2), (rows, count), 0, 4096) + boost
    holders = jax.random.permutation(jax.random.fold_in(rng, 3), rows)[jnp.arange(count) % rows]
    chance = jnp.where(jnp.arange(rows)[:, None] == holders[None, :], 1 << 14, chance)
    score = chance * count + jnp.arange(count)
    return lax.top_k(score.astype(jnp.int32), top)[1].astype(jnp.int32)


def gaussian(own_key, extent, scale, reach, pieces=(), held_as=jnp.bfloat16):
    array = jax.random.normal(own_key, extent, jnp.float32) * scale
    if len(pieces) > 0:
        array = shard_levels(own_key, extent, pieces, -0.22, 0.18) * array
    return jnp.clip(array, min=-reach, max=reach).astype(held_as)


def setup_inputs(seed: int = 0) -> dict:
    streams_of = jax.random.split(jax.random.key(seed), 9)
    return {
        "inputs": gaussian(streams_of[0], (TOKENS, D), 1.0, 6.0, ((0, 32),), jnp.float32),
        "cotangent": gaussian(streams_of[1], (TOKENS, D), 1.0, 6.0, ((0, 32),), jnp.float32),
        "up_blocks": gaussian(streams_of[2], (FFB, KB, BLK, BLK), (KB * BLK) ** -0.5, 0.25, ((0, 8), (2, 32)), jnp.float32),
        "down_blocks": gaussian(streams_of[3], (FFB, KB, BLK, BLK), (KB * BLK) ** -0.5, 0.25, ((0, 8), (2, 32)), jnp.float32),
        "up_index": picks_of(streams_of[4], FFB, D // BLK, KB, 0),
        "down_index": picks_of(streams_of[5], FFB, D // BLK, KB, 0),
        "mom_up": gaussian(streams_of[6], (FFB, KB, BLK, BLK), 1.0, 6.0, ((0, 8), (2, 32)), jnp.float32),
        "mom_down": gaussian(streams_of[7], (FFB, KB, BLK, BLK), 1.0, 6.0, ((0, 8), (2, 32)), jnp.float32),
    }


def reference(inputs, cotangent, up_blocks, down_blocks, up_index, down_index, mom_up, mom_down):
    token_count = inputs.shape[0]
    block = up_blocks.shape[2]
    x_blocks = inputs.reshape(token_count, -1, block)
    cot_blocks = cotangent.reshape(token_count, -1, block)
    grad_scale = token_count ** -0.5
    highest = lax.Precision.HIGHEST

    def block_step(carried, scan_item):
        w_up, w_down, up_row, down_row = scan_item
        x_sel = jnp.take(x_blocks, up_row.astype(jnp.int32), axis=1)
        cot_sel = jnp.take(cot_blocks, down_row.astype(jnp.int32), axis=1)
        pre_act = jnp.einsum('tkd,kdc->tc', x_sel, w_up, precision=highest)
        sigmoid_pre = jax.nn.sigmoid(pre_act)
        activation = pre_act * sigmoid_pre
        grad_act = jnp.einsum('tkd,kcd->tc', cot_sel, w_down, precision=highest)
        grad_pre = grad_act * sigmoid_pre * (1.0 + pre_act * (1.0 - sigmoid_pre))
        back_terms = jnp.einsum('tc,kdc->tkd', grad_pre, w_up, precision=highest)
        carried = carried.at[:, up_row.astype(jnp.int32)].add(back_terms)
        grad_up = grad_scale * jnp.einsum('tkd,tc->kdc', x_sel, grad_pre, precision=highest)
        grad_down = grad_scale * jnp.einsum('tc,tkd->kcd', activation, cot_sel, precision=highest)
        return carried, (grad_up, grad_down)

    start_grad = jnp.zeros(x_blocks.shape, jnp.float32)
    input_grad, (grad_up, grad_down) = lax.scan(block_step, start_grad, (up_blocks, down_blocks, up_index, down_index))
    return input_grad.reshape(token_count, -1), 0.9 * mom_up + grad_up, 0.9 * mom_down + grad_down
```

```python
import functools

import jax
import jax.numpy as jnp
from jax import lax
from jax.experimental import pallas as pl
from jax.experimental.pallas import tpu as pltpu
from jax.sharding import PartitionSpec as P

MESH = pl.DeviceIdType.MESH
NX, NY, NZ = 4, 4, 8
NF = 7
NA = 3
BF, F32 = jnp.bfloat16, jnp.float32


def split(a):
    hi = a.astype(BF)
    return hi, (a - hi.astype(F32)).astype(BF)


def dot3(a, b, dims):
    ah, al = a
    bh, bl = b
    d = functools.partial(lax.dot_general, dimension_numbers=(dims, ((), ())), preferred_element_type=F32)
    return d(ah, bh) + d(ah, bl) + d(al, bh)


def merge4(lo, a, b):
    ra, rb = pltpu.roll(a, 4, 1), pltpu.roll(b, 4, 1)
    return jnp.where(lo, a, rb), jnp.where(lo, ra, b)


def kernel(
    ui, di, slot, x_h, c_h, up_h, dn_h, mu_h, md_h,
    ig_out, mu_out, md_out,
    xo, xp, w, g, act, gpre, terms, ig,
    rau, rad, rbu, rbd, rx, rax, rc, cs, ryu, ryd, rp, mom,
    lsem, ssem, rsem,
):
    t, h = lax.axis_index("tok"), lax.axis_index("hid")
    z, x = t // NX, lax.rem(t, NX)
    y, c = h // 2, lax.rem(h, 2)
    hf = x // 2
    j = jnp.where((x == 1) | (x == 2), 1, 0)
    zz = lambda d: lax.rem(z + d + NZ, NZ)
    yy = lambda d: lax.rem(y + d + NY, NY)
    tok = lambda tz, tx: tz * NX + tx
    cross = (tok(z, 3 - x), h)
    inhalf = (tok(z, x + 1 - 2 * lax.rem(x, 2)), h)
    zup, zdn = (tok(zz(1), x), h), (tok(zz(-1), x), h)
    yup, ydn = (t, yy(1) * 2 + c), (t, yy(-1) * 2 + c)
    sib = (t, y * 2 + 1 - c)

    barrier = pltpu.get_barrier_semaphore()
    for dev in (cross, inhalf, zup, zdn, yup, ydn, sib):
        pl.semaphore_signal(barrier, inc=1, device_id=dev, device_id_type=MESH)

    nloc = [0]
    nrem = [0]
    pending = []

    def local(src, dst):
        cp = pltpu.make_async_copy(src, dst, lsem.at[nloc[0]])
        nloc[0] += 1
        cp.start()
        return cp

    def send(src, dst, dev, arrive=None):
        n = nrem[0]
        nrem[0] += 1
        cp = pltpu.make_async_remote_copy(src, dst, ssem.at[n], rsem.at[n], device_id=dev, device_id_type=MESH)
        cp.start()
        pending.append(cp)
        arrive = dst if arrive is None else arrive
        return pltpu.make_async_remote_copy(arrive, arrive, ssem.at[n], rsem.at[n], device_id=dev, device_id_type=MESH)

    lw = [
        local(up_h.at[pl.ds(NF * hf, NF)], w.at[z, j, hf, 0]),
        local(dn_h.at[pl.ds(NF * hf, NF)], w.at[z, j, hf, 1]),
    ]
    lx = [local(x_h, xo.at[0]), local(c_h, xo.at[1])]
    lm = [local(mu_h, mom.at[0]), local(md_h, mom.at[1])]

    pl.semaphore_wait(barrier, 7)

    oh = NF * (1 - hf)
    w0 = []
    for lo_f, n_f in ((0, NA), (NA, NF - NA)):
        for m, ref in enumerate((up_h, dn_h)):
            w0.append(
                send(
                    ref.at[pl.ds(oh + lo_f, n_f)],
                    w.at[z, j, hf, m, pl.ds(lo_f, n_f)],
                    cross,
                    w.at[z, j, 1 - hf, m, pl.ds(lo_f, n_f)],
                )
            )
    wa = lambda tz: w.at[tz, :, :, :, pl.ds(0, NA)]
    wah = lambda tz, jj: w.at[tz, jj, :, :, pl.ds(0, NA)]
    wb = lambda tz, jj: w.at[tz, jj, :, :, pl.ds(NA, NF - NA)]
    wbh = lambda tz, jj, m: w.at[tz, jj, m, :, pl.ds(NA, NF - NA)]

    tchunks = [(m, r) for m in range(2) for r in range(2)]
    RH = 8

    def share(m, r, ty, tc, sub=None):
        rows = pl.ds(r * RH, RH) if sub is None else pl.ds(r * RH + sub * (RH // 2), RH // 2)
        return xp.at[m, rows, pl.ds((tc * NY + ty) * 4, 4)]

    t0 = []
    for m, r in tchunks:
        src = (x_h, c_h)[m].at[pl.ds(r * RH, RH), pl.ds((c * NY + y) * 4, 4)]
        t0.append(send(src, share(m, r, y, c), cross))

    az, bz, bx, ty, tc = {}, {}, [], {}, []

    def a_ring(s):
        if s < NZ // 2 - 1:
            az[s] = (
                send(wa(zz(-s)), wa(zz(-s)), zup, wa(zz(-1 - s))),
                send(wa(zz(s)), wa(zz(s)), zdn, wa(zz(1 + s))),
            )
        else:
            az[s] = (
                send(wah(zz(-s), 0), wah(zz(-s), 0), zup, wah(zz(-1 - s), 0)),
                send(wah(zz(s), 1), wah(zz(s), 1), zdn, wah(zz(1 + s), 1)),
            )

    def b_ring(s):
        if s < NZ // 2 - 1:
            bz[s] = (
                send(wb(zz(-s), j), wb(zz(-s), j), zup, wb(zz(-1 - s), j)),
                send(wb(zz(s), j), wb(zz(s), j), zdn, wb(zz(1 + s), j)),
            )
        else:
            bz[s] = (
                send(wbh(zz(-s), j, 0), wbh(zz(-s), j, 0), zup, wbh(zz(-1 - s), j, 0)),
                send(wbh(zz(s), j, 1), wbh(zz(s), j, 1), zdn, wbh(zz(1 + s), j, 1)),
            )

    def b_x(d):
        bx.append(send(wb(zz(d), j), wb(zz(d), j), inhalf, wb(zz(d), 1 - j)))

    def t_core(k, d):
        m, r = tchunks[k]
        tc.append(send(share(m, r, yy(d), c), share(m, r, yy(d), c), sib, share(m, r, yy(d), 1 - c)))

    def t_ring(k, s):
        m, r = tchunks[k]
        if s == 0:
            ty[k, s] = (
                send(share(m, r, y, c), share(m, r, y, c), yup, share(m, r, yy(-1), c)),
                send(share(m, r, y, c), share(m, r, y, c), ydn, share(m, r, yy(1), c)),
            )
        else:
            ty[k, s] = (
                send(share(m, r, yy(-1), c, 0), share(m, r, yy(-1), c, 0), yup, share(m, r, yy(-2), c, 0)),
                send(share(m, r, yy(1), c, 1), share(m, r, yy(1), c, 1), ydn, share(m, r, yy(2), c, 1)),
            )

    def got(pair):
        for cp in pair:
            cp.wait_recv()

    def tok_own(k):
        t0[k].wait_recv()
        t_ring(k, 0)
        t_core(k, 0)

    def tok_mid(k):
        got(ty[k, 0])
        t_ring(k, 1)
        t_core(k, -1)
        t_core(k, 1)

    def tok_last(k):
        got(ty[k, 1])
        t_core(k, 2)

    def b_mid(s):
        got(bz[s])
        b_ring(s + 1)
        b_x(-1 - s)
        b_x(1 + s)

    def a_mid(s):
        got(az[s])
        a_ring(s + 1)

    for cp in lw:
        cp.wait()
    got(w0[:2])
    ax = send(wah(z, j), wah(z, j), inhalf, wah(z, 1 - j))
    got(w0[2:])
    b_ring(0)
    b_x(0)
    ax.wait_recv()
    a_ring(0)
    tok_own(0)
    b_mid(0)
    tok_own(1)
    a_mid(0)
    tok_own(2)
    tok_mid(0)
    b_mid(1)
    tok_own(3)
    a_mid(1)
    tok_mid(1)
    b_mid(2)
    tok_last(0)
    tok_mid(2)
    a_mid(2)
    tok_last(1)
    tok_mid(3)
    tok_last(2)
    got(bz[NZ // 2 - 1])
    b_x(NZ // 2)
    tok_last(3)
    got(az[NZ // 2 - 1])
    got(bx)
    got(tc)
    for cp in lx:
        cp.wait()

    lo = lax.broadcasted_iota(jnp.int32, (NZ, 8, 128), 1) < 4

    def weights(m, i):
        out = []
        for kp in range(2):
            x0, x3, x1, x2 = (w[:, jj, mm, m, i, kp] for jj in range(2) for mm in range(2))
            a0, b0 = merge4(lo, x0, x1)
            a1, b1 = merge4(lo, x2, x3)
            out += [jnp.stack([a0, a1], 1).reshape(128, 128), jnp.stack([b0, b1], 1).reshape(128, 128)]
        return out

    def tokens(m, idx, i):
        cols = []
        for k in range(4):
            b = idx[NF * hf + i, k]
            cols.append(jnp.concatenate([xo[m, :, b].reshape(128, 128), xp[m, :, b].reshape(128, 128)], 0))
        return split(jnp.concatenate(cols, 1))

    def forward(i, carry):
        wu = split(jnp.concatenate(weights(0, i), 0))
        wd = split(jnp.concatenate(weights(1, i), 1))
        pre = dot3(tokens(0, ui, i), wu, ((1,), (0,)))
        ga = dot3(tokens(1, di, i), wd, ((1,), (1,)))
        sg = 1.0 / (1.0 + jnp.exp(-pre))
        act[i] = pre * sg
        gp = ga * sg * (1.0 + pre * (1.0 - sg))
        gpre[i] = gp
        back = dot3(split(gp), wu, ((1,), (1,)))
        for k in range(4):
            terms[i * 4 + k] = back[:, k * 128 : (k + 1) * 128]
        return carry

    terms[4 * NF] = jnp.zeros((256, 128), F32)
    lax.fori_loop(0, NF, forward, 0)

    def gather_terms(b, carry):
        total = terms[slot[NF * hf, b]]
        for i in range(1, NF):
            total = total + terms[slot[NF * hf + i, b]]
        ig[b // 8, lax.rem(b // 4, 2), lax.rem(b, 4)] = total
        return carry

    lax.fori_loop(0, 32, gather_terms, 0)

    yorder = (2, 1, -1, 0)
    core = [send(ig.at[yy(d), 1 - c], cs.at[n], sib) for n, d in enumerate(yorder)]

    def grads(i, carry):
        gp = split(gpre[i])
        ac = split(act[i])
        gu = dot3(tokens(0, ui, i), gp, ((0,), (0,)))
        gd = dot3(ac, tokens(1, di, i), ((0,), (0,)))
        for m, full in enumerate((gu, gd)):
            for kp in range(2):
                if m == 0:
                    k0, k1 = (full[(2 * kp + e) * 128 : (2 * kp + e + 1) * 128] for e in range(2))
                else:
                    k0, k1 = (full[:, (2 * kp + e) * 128 : (2 * kp + e + 1) * 128] for e in range(2))
                k0, k1 = k0.reshape(NZ, 2, 8, 128), k1.reshape(NZ, 2, 8, 128)
                x0, x1 = merge4(lo, k0[:, 0], k1[:, 0])
                x2, x3 = merge4(lo, k0[:, 1], k1[:, 1])
                g[:, 0, 0, m, i, kp] = x0
                g[:, 1, 0, m, i, kp] = x1
                g[:, 1, 1, m, i, kp] = x2
                g[:, 0, 1, m, i, kp] = x3
        return carry

    lax.fori_loop(0, NF, grads, 0)

    A, B = pl.ds(0, NA), pl.ds(NA, NF - NA)
    zorder = [NZ // 2]
    for d in range(NZ // 2 - 1, 0, -1):
        zorder += [d, -d]
    zorder.append(0)
    xs = {d: send(g.at[zz(d), 1 - j, :, :, B], rx.at[n], inhalf) for n, d in enumerate(zorder)}
    ar, br, yr = {}, {}, {}

    def ra_ring(s):
        d = NZ // 2 - s
        if s == 0:
            ar[s] = (
                send(g.at[zz(d), 0, :, :, A], rau.at[0, 0], zup),
                send(g.at[zz(-d), 1, :, :, A], rad.at[0, 1], zdn),
            )
            return
        got(ar[s - 1])
        if s == 1:
            g[zz(d), 0, :, :, A] += rau[0, 0]
            g[zz(-d), 1, :, :, A] += rad[0, 1]
        else:
            g[zz(d), :, :, :, A] += rau[s - 1]
            g[zz(-d), :, :, :, A] += rad[s - 1]
        ar[s] = (
            send(g.at[zz(d), :, :, :, A], rau.at[s], zup),
            send(g.at[zz(-d), :, :, :, A], rad.at[s], zdn),
        )

    def add_x(d):
        xs[d].wait_recv()
        g[zz(d), j, :, :, B] += rx[zorder.index(d)]

    def rb_ring(s):
        d = NZ // 2 - s
        add_x(d)
        if s == 0:
            br[s] = (
                send(g.at[zz(d), j, 0, :, B], rbu.at[0, 0], zup),
                send(g.at[zz(-d), j, 1, :, B], rbd.at[0, 1], zdn),
            )
            return
        add_x(-d)
        got(br[s - 1])
        if s == 1:
            g[zz(d), j, 0, :, B] += rbu[0, 0]
            g[zz(-d), j, 1, :, B] += rbd[0, 1]
        else:
            g[zz(d), j, :, :, B] += rbu[s - 1]
            g[zz(-d), j, :, :, B] += rbd[s - 1]
        br[s] = (
            send(g.at[zz(d), j, :, :, B], rbu.at[s], zup),
            send(g.at[zz(-d), j, :, :, B], rbd.at[s], zdn),
        )

    def add_core(n):
        core[n].wait_recv()
        for b in range(4):
            ig[yy(yorder[n]), c, b] += cs[n, b]

    ra_ring(0)
    add_core(0)
    yr[0] = (
        send(ig.at[yy(2), c, pl.ds(0, 2)], ryu.at[0, pl.ds(0, 2)], yup),
        send(ig.at[yy(-2), c, pl.ds(2, 2)], ryd.at[0, pl.ds(2, 2)], ydn),
    )
    rb_ring(0)
    ra_ring(1)
    add_core(1)
    add_core(2)
    got(yr[0])
    for b in range(2):
        ig[yy(1), c, b] += ryu[0, b]
        ig[yy(-1), c, 2 + b] += ryd[0, 2 + b]
    yr[1] = (
        send(ig.at[yy(1), c], ryu.at[1], yup),
        send(ig.at[yy(-1), c], ryd.at[1], ydn),
    )
    rb_ring(1)
    ra_ring(2)
    add_core(3)
    rb_ring(2)
    ra_ring(3)
    got(yr[1])
    for b in range(4):
        ig[y, c, b] += ryu[1, b] + ryd[1, b]
    pair = send(ig.at[y, c, :, pl.ds(128, 128)], rp, cross)
    rb_ring(3)
    last = NZ // 2 - 1
    got(ar[last])
    g[z, :, :, :, A] += rau[last] + rad[last]
    axs = send(g.at[z, 1 - j, :, :, A], rax, inhalf)
    pair.wait_recv()
    for b in range(4):
        ig_out[:, b * 128 : (b + 1) * 128] = ig[y, c, b, 0:128] + rp[b]
    axs.wait_recv()
    g[z, j, :, :, A] += rax[...]
    ca = send(g.at[z, j, 1 - hf, :, A], rc.at[:, A], cross)
    add_x(0)
    got(br[last])
    g[z, j, :, :, B] += rbu[last] + rbd[last]
    cb = send(g.at[z, j, 1 - hf, :, B], rc.at[:, B], cross)
    for cp in lm:
        cp.wait()
    scale = 1.0 / 64.0
    for m, out in enumerate((mu_out, md_out)):
        out[pl.ds(NF * hf, NF)] = 0.9 * mom[m, pl.ds(NF * hf, NF)] + scale * g[z, j, hf, m]
    ca.wait_recv()
    cb.wait_recv()
    for m, out in enumerate((mu_out, md_out)):
        out[pl.ds(oh, NF)] = 0.9 * mom[m, pl.ds(oh, NF)] + scale * rc[m]
    for cp in pending:
        cp.wait_send()


def shards(inputs, cotangent, up_blocks, down_blocks, up_index, down_index, mom_up, mom_down):
    f, kb, r, b = up_blocks.shape
    tiles = lambda a: a.reshape(f, kb // 2, 2 * r, b)
    hit = up_index[:, :, None] == jnp.arange(32, dtype=jnp.int32)
    pos = 4 * (jnp.arange(f, dtype=jnp.int32) % NF)[:, None, None] + jnp.arange(kb, dtype=jnp.int32)[None, :, None]
    slot = jnp.min(jnp.where(hit, pos, 4 * NF), axis=1)
    rows8 = lambda a: a.reshape(16, 8, 32, b).transpose(0, 2, 1, 3)
    vm = lambda *s: pltpu.VMEM(s, F32)
    hbm, smem = pl.BlockSpec(memory_space=pl.ANY), pl.BlockSpec(memory_space=pltpu.SMEM)
    vmem = pl.BlockSpec(memory_space=pltpu.VMEM)
    tile = (2, 8, 128)
    ig, mu, md = pl.pallas_call(
        kernel,
        out_shape=(
            jax.ShapeDtypeStruct((128, 512), F32),
            jax.ShapeDtypeStruct((f, *tile), F32),
            jax.ShapeDtypeStruct((f, *tile), F32),
        ),
        in_specs=[smem] * 3 + [hbm] * 6,
        out_specs=(vmem, vmem, vmem),
        scratch_shapes=[
            vm(2, 16, 32, 8, 128),
            vm(2, 16, 32, 8, 128),
            vm(NZ, 2, 2, 2, NF, *tile),
            vm(NZ, 2, 2, 2, NF, *tile),
            vm(NF, 256, 128),
            vm(NF, 256, 128),
            vm(4 * NF + 1, 256, 128),
            vm(NY, 2, 4, 256, 128),
            vm(NZ // 2, 2, 2, 2, NA, *tile),
            vm(NZ // 2, 2, 2, 2, NA, *tile),
            vm(NZ // 2, 2, 2, NF - NA, *tile),
            vm(NZ // 2, 2, 2, NF - NA, *tile),
            vm(NZ, 2, 2, NF - NA, *tile),
            vm(2, 2, NA, *tile),
            vm(2, NF, *tile),
            vm(NY, 4, 256, 128),
            vm(2, 4, 256, 128),
            vm(2, 4, 256, 128),
            vm(4, 128, 128),
            vm(2, f, *tile),
            pltpu.SemaphoreType.DMA((6,)),
            pltpu.SemaphoreType.DMA((112,)),
            pltpu.SemaphoreType.DMA((112,)),
        ],
        compiler_params=pltpu.CompilerParams(
            collective_id=0, has_side_effects=True, vmem_limit_bytes=60 * 1024 * 1024
        ),
    )(up_index, down_index, slot, rows8(inputs), rows8(cotangent), tiles(up_blocks), tiles(down_blocks), tiles(mom_up), tiles(mom_down))
    return ig, mu.reshape(mom_up.shape), md.reshape(mom_down.shape)


def solution(mesh):
    return jax.shard_map(
        shards,
        mesh=mesh,
        in_specs=(
            P("tok", None),
            P("tok", None),
            P("hid", None, "tok", None),
            P("hid", None, "tok", None),
            P("hid", None),
            P("hid", None),
            P("hid", None, "tok", None),
            P("hid", None, "tok", None),
        ),
        out_specs=(P("tok", "hid"), P("hid", None, "tok", None), P("hid", None, "tok", None)),
        check_vma=False,
    )
```

```python
import functools
import heapq

import jax
import jax.numpy as jnp
from jax import lax
from jax.experimental import pallas as pl
from jax.experimental.pallas import tpu as pltpu
from jax.sharding import PartitionSpec as P

MESH = pl.DeviceIdType.MESH
NX, NY, NZ = 4, 4, 8
NF = 7
NA = 3
BF, F32 = jnp.bfloat16, jnp.float32


def split(a):
    hi = a.astype(BF)
    return hi, (a - hi.astype(F32)).astype(BF)


def dot3(a, b, dims):
    ah, al = a
    bh, bl = b
    d = functools.partial(lax.dot_general, dimension_numbers=(dims, ((), ())), preferred_element_type=F32)
    return d(ah, bh) + d(ah, bl) + d(al, bh)


def merge4(lo, a, b):
    ra, rb = pltpu.roll(a, 4, 1), pltpu.roll(b, 4, 1)
    return jnp.where(lo, a, rb), jnp.where(lo, ra, b)


class Plan:
    RATE = {"core": 250.0}
    LAT = {"core": 1.0, "cross": 1.9, "in": 1.9, "yu": 1.9, "yd": 1.9, "zu": 2.2, "zd": 2.2}

    def __init__(self, ssem, rsem, devs):
        self.ssem, self.rsem, self.devs = ssem, rsem, devs
        self.items, self.sent = [], []

    def send(self, name, link, src, dst, arrive, size, deps=(), land=None, before=None):
        self.items.append(dict(name=name, link=link, src=src, dst=dst, arrive=arrive, size=size, deps=set(deps), land=land, before=before))

    def step(self, name, cost, fn, deps=()):
        self.items.append(dict(name=name, link=None, cost=cost, fn=fn, deps=set(deps)))

    def issue(self, it):
        n = len(self.sent)
        if it["before"] is not None:
            it["before"]()
        mk = lambda s, d: pltpu.make_async_remote_copy(
            s, d, self.ssem.at[n], self.rsem.at[n], device_id=self.devs[it["link"]], device_id_type=MESH
        )
        cp = mk(it["src"], it["dst"])
        cp.start()
        self.sent.append(cp)
        return mk(it["arrive"], it["arrive"])

    def run(self):
        now, free, done, flying, todo, tick = 0.0, {}, set(), [], list(self.items), 0
        while todo or flying:
            for it in [i for i in todo if i["link"] and i["deps"] <= done]:
                todo.remove(it)
                handle = self.issue(it)
                end = max(now, free.get(it["link"], 0.0)) + it["size"] / 1e3 / self.RATE.get(it["link"], 46.0)
                free[it["link"]] = end
                heapq.heappush(flying, (end + self.LAT[it["link"]], tick, it, handle))
                tick += 1
            ready = next((i for i in todo if not i["link"] and i["deps"] <= done), None)
            if ready is not None and not (flying and flying[0][0] <= now):
                todo.remove(ready)
                ready["fn"]()
                now += ready["cost"]
                done.add(ready["name"])
                continue
            when, _, it, handle = heapq.heappop(flying)
            now = max(now, when)
            handle.wait_recv()
            if it["land"] is not None:
                it["land"]()
            done.add(it["name"])
        for cp in self.sent:
            cp.wait_send()


def kernel(
    ui, di, x_h, c_h, up_h, dn_h,
    ig_out, gu_out, gd_out,
    xo, xp, w, g, act, gpre, terms, ig,
    rau, rad, rbu, rbd, rx, rax, rc, cs, ryu, ryd, rp, slot,
    lsem, ssem, rsem,
):
    t, h = lax.axis_index("tok"), lax.axis_index("hid")
    z, x = t // NX, lax.rem(t, NX)
    y, c = h // 2, lax.rem(h, 2)
    hf = x // 2
    j = jnp.where((x == 1) | (x == 2), 1, 0)
    zz = lambda d: lax.rem(z + d + NZ, NZ)
    yy = lambda d: lax.rem(y + d + NY, NY)
    tok = lambda tz, tx: tz * NX + tx
    devs = {
        "cross": (tok(z, 3 - x), h),
        "in": (tok(z, x + 1 - 2 * lax.rem(x, 2)), h),
        "zu": (tok(zz(1), x), h),
        "zd": (tok(zz(-1), x), h),
        "yu": (t, yy(1) * 2 + c),
        "yd": (t, yy(-1) * 2 + c),
        "core": (t, y * 2 + 1 - c),
    }
    barrier = pltpu.get_barrier_semaphore()
    for dev in devs.values():
        pl.semaphore_signal(barrier, inc=1, device_id=dev, device_id_type=MESH)

    def local(n, src, dst):
        cp = pltpu.make_async_copy(src, dst, lsem.at[n])
        cp.start()
        return cp

    lw = [
        local(0, up_h.at[pl.ds(NF * hf, NF)], w.at[z, j, hf, 0]),
        local(1, dn_h.at[pl.ds(NF * hf, NF)], w.at[z, j, hf, 1]),
    ]
    lx = [local(2, x_h, xo.at[0]), local(3, c_h, xo.at[1])]
    for cp in lw:
        cp.wait()
    pl.semaphore_wait(barrier, len(devs))

    p = Plan(ssem, rsem, devs)
    A, B = pl.ds(0, NA), pl.ds(NA, NF - NA)
    KA, KB = NA * 16.384, (NF - NA) * 16.384
    KA, KB = KA * 1e3, KB * 1e3
    HZ = NZ // 2
    js, ms = (j, 1 - j), (hf, 1 - hf)
    oh = NF * (1 - hf)

    wA = lambda d, a, m: w.at[zz(d), js[a], ms[m], :, A]
    wB = lambda d, a, m: w.at[zz(d), js[a], ms[m], :, B]
    need_w = []

    def gather_ring(tag, ref, size, m, deps0):
        have = {0: deps0}
        for s in range(HZ):
            for link, sg in (("zu", -1), ("zd", 1)):
                if s == HZ - 1 and (m == 0) != (link == "zu"):
                    continue
                name = f"{tag}{m}{link}{s}"
                p.send(name, link, ref(sg * s), ref(sg * s), ref(sg * (s + 1)), size, have[sg * s])
                have[HZ if s == HZ - 1 else sg * (s + 1)] = [name]
                need_w.append(name)
        return have

    for m in range(2):
        p.send(f"ax{m}", "in", wA(0, 0, m), wA(0, 0, m), wA(0, 1, m), KA, [] if m == 0 else ["w0a0", "w0a1"])
        need_w.append(f"ax{m}")
        hb = gather_ring("b", lambda d, m=m: wB(d, 0, m), KB, m, [] if m == 0 else ["w0b0", "w0b1"])
        for d in (0, -1, 1, -2, 2, -3, 3, HZ):
            p.send(f"bx{m}{d}", "in", wB(d, 0, m), wB(d, 0, m), wB(d, 1, m), KB, hb[d])
            need_w.append(f"bx{m}{d}")
        gather_ring("a", lambda d, m=m: wA(d, 0, m), KA, m, [] if m == 0 else ["w0a0", "w0a1"])
        gather_ring("o", lambda d, m=m: wA(d, 1, m), KA, m, [f"ax{m}"])
        if m == 0:
            for tag, F, lo_f, n_f in (("b", B, NA, NF - NA), ("a", A, 0, NA)):
                for q, ref in enumerate((up_h, dn_h)):
                    p.send(
                        f"w0{tag}{q}", "cross", ref.at[pl.ds(oh + lo_f, n_f)],
                        w.at[z, j, hf, q, F], w.at[z, j, 1 - hf, q, F], n_f * 8192,
                    )

    RH = 4
    need_t = []
    KT = RH * 8 * 512 * 4

    def share(m, r, ty, tc, sub=None):
        rows = pl.ds(r * RH, RH) if sub is None else pl.ds(r * RH + sub * (RH // 2), RH // 2)
        return xp.at[m, rows, pl.ds((tc * NY + ty) * 4, 4)]

    for m in range(2):
        for r in range(16 // RH):
            k = f"{m}{r}"
            sh = lambda d, q=c, sub=None, m=m, r=r: share(m, r, yy(d), q, sub)
            src = (x_h, c_h)[m].at[pl.ds(r * RH, RH), pl.ds((c * NY + y) * 4, 4)]
            p.send(f"t{k}", "cross", src, sh(0), sh(0), KT)
            p.send(f"tyu{k}", "yu", sh(0), sh(0), sh(-1), KT, [f"t{k}"])
            p.send(f"tyd{k}", "yd", sh(0), sh(0), sh(1), KT, [f"t{k}"])
            p.send(f"tzu{k}", "yu", sh(-1, c, 0), sh(-1, c, 0), sh(-2, c, 0), KT // 2, [f"tyu{k}"])
            p.send(f"tzd{k}", "yd", sh(1, c, 1), sh(1, c, 1), sh(2, c, 1), KT // 2, [f"tyd{k}"])
            for d, dep in ((0, [f"t{k}"]), (-1, [f"tyu{k}"]), (1, [f"tyd{k}"]), (2, [f"tzu{k}", f"tzd{k}"])):
                p.send(f"tc{k}{d}", "core", sh(d), sh(d), sh(d, 1 - c), KT, dep)
                need_t.append(f"tc{k}{d}")

    def make_slots():
        for i in range(NF):
            picks = [ui[k, NF * hf + i] for k in range(4)]

            def one(b, carry, i=i, picks=picks):
                v = jnp.int32(4 * NF)
                for k in range(4):
                    v = jnp.where(picks[k] == b, 4 * i + k, v)
                slot[i, b] = v
                return carry

            lax.fori_loop(0, 32, one, 0)
        terms[4 * NF] = jnp.zeros((256, 128), F32)

    p.step("slots", 0.5, make_slots)
    lo = lax.broadcasted_iota(jnp.int32, (NZ, 8, 128), 1) < 4

    def weights(m, i):
        out = []
        for kp in range(2):
            x0, x3, x1, x2 = (w[:, jj, mm, m, i, kp] for jj in range(2) for mm in range(2))
            a0, b0 = merge4(lo, x0, x1)
            a1, b1 = merge4(lo, x2, x3)
            out += [jnp.stack([a0, a1], 1).reshape(128, 128), jnp.stack([b0, b1], 1).reshape(128, 128)]
        return out

    def tokens(m, idx, i):
        cols = []
        for k in range(4):
            b = idx[k, NF * hf + i]
            cols.append(jnp.concatenate([xo[m, :, b].reshape(128, 128), xp[m, :, b].reshape(128, 128)], 0))
        return split(jnp.concatenate(cols, 1))

    def forward(i, carry):
        wu = split(jnp.concatenate(weights(0, i), 0))
        wd = split(jnp.concatenate(weights(1, i), 1))
        pre = dot3(tokens(0, ui, i), wu, ((1,), (0,)))
        ga = dot3(tokens(1, di, i), wd, ((1,), (1,)))
        sg = 1.0 / (1.0 + jnp.exp(-pre))
        act[i] = pre * sg
        gp = ga * sg * (1.0 + pre * (1.0 - sg))
        gpre[i] = gp
        back = dot3(split(gp), wu, ((1,), (1,)))
        for k in range(4):
            terms[i * 4 + k] = back[:, k * 128 : (k + 1) * 128]
        return carry

    def gather_terms(b, carry):
        total = terms[slot[0, b]]
        for i in range(1, NF):
            total = total + terms[slot[i, b]]
        ig[b // 8, lax.rem(b // 4, 2), lax.rem(b, 4)] = total
        return carry

    def grads(i, carry):
        gp = split(gpre[i])
        ac = split(act[i])
        gu = dot3(tokens(0, ui, i), gp, ((0,), (0,)))
        gd = dot3(ac, tokens(1, di, i), ((0,), (0,)))
        for m, full in enumerate((gu, gd)):
            for kp in range(2):
                if m == 0:
                    k0, k1 = (full[(2 * kp + e) * 128 : (2 * kp + e + 1) * 128] for e in range(2))
                else:
                    k0, k1 = (full[:, (2 * kp + e) * 128 : (2 * kp + e + 1) * 128] for e in range(2))
                k0, k1 = k0.reshape(NZ, 2, 8, 128), k1.reshape(NZ, 2, 8, 128)
                x0, x1 = merge4(lo, k0[:, 0], k1[:, 0])
                x2, x3 = merge4(lo, k0[:, 1], k1[:, 1])
                g[:, 0, 0, m, i, kp] = x0
                g[:, 1, 0, m, i, kp] = x1
                g[:, 1, 1, m, i, kp] = x2
                g[:, 0, 1, m, i, kp] = x3
        return carry

    loop = lambda a, b, fn: lambda: lax.fori_loop(a, b, fn, 0) and None

    def wait_own():
        for cp in lx:
            cp.wait()

    p.step("own", 0.1, wait_own)
    p.step("fwd", 9.0, loop(0, NF, forward), need_w + need_t + ["own", "slots"])
    p.step("terms", 0.5, loop(0, 32, gather_terms), ["fwd"])

    KI = 2 * 256 * 128 * 4
    P2 = lambda b: pl.ds(2 * b, 2)

    def add_ig(d, b, buf):
        def fn():
            for e in range(2):
                ig[yy(d), c, 2 * b + e] += buf[e]

        return fn

    for n, d in enumerate((2, 1, -1, 0)):
        for b in range(2):
            p.send(
                f"c{d}{b}", "core", ig.at[yy(d), 1 - c, P2(b)], cs.at[n, P2(b)], cs.at[n, P2(b)], KI,
                ["terms"], add_ig(d, b, cs.at[n, P2(b)]),
            )
    for b in range(2):
        for link, sg, buf in (("yu", 1, ryu), ("yd", -1, ryd)):
            dep = [f"c{sg}{b}"]
            if (b == 0) == (link == "yu"):
                p.send(
                    f"y2{b}", link, ig.at[yy(2), c, P2(b)], buf.at[0, P2(b)], buf.at[0, P2(b)], KI, [f"c2{b}"],
                )
                dep.append(f"y2{b}")
                before = add_ig(sg, b, buf.at[0, P2(b)])
            else:
                before = None
            p.send(
                f"y1{link}{b}", link, ig.at[yy(sg), c, P2(b)], buf.at[1, P2(b)], buf.at[1, P2(b)], KI, dep,
                None, before,
            )

    def ig_sum(b):
        def fn():
            for e in range(2 * b, 2 * b + 2):
                ig[y, c, e] += ryu[1, e] + ryd[1, e]

        return fn

    def ig_final(b):
        def fn():
            for e in range(2 * b, 2 * b + 2):
                ig_out[:, e * 128 : (e + 1) * 128] = ig[y, c, e, 0:128] + rp[e]

        return fn

    for b in range(2):
        p.send(
            f"p{b}", "cross", ig.at[y, c, P2(b), pl.ds(128, 128)], rp.at[P2(b)], rp.at[P2(b)], KI // 2,
            [f"y1yu{b}", f"y1yd{b}", f"c0{b}"], ig_final(b), ig_sum(b),
        )

    p.step("gB", 2.1, loop(NA, NF, grads), ["terms"])
    p.step("gA", 1.6, loop(0, NA, grads), ["gB"])

    zorder = (HZ, 3, -3, 2, -2, 1, -1, 0)

    def add_to(ref, buf):
        def fn():
            ref[...] += buf[...]

        return fn

    gA = lambda d, a, m: g.at[zz(d), js[a], ms[m], :, A]
    gB = lambda d, a, m: g.at[zz(d), js[a], ms[m], :, B]
    for n, d in enumerate(zorder):
        for m in range(2):
            buf = rx.at[n, ms[m]]
            p.send(f"rx{m}{d}", "in", gB(d, 1, m), buf, buf, KB, ["gB"], add_to(gB(d, 0, m), buf))

    def reduce_ring(tag, ref, bufs, size, m, deps):
        for s in range(HZ):
            for link, sg in (("zu", 1), ("zd", -1)):
                if s == 0 and (m == 0) != (link == "zu"):
                    continue
                d = sg * (HZ - s)
                dep, before = list(deps(HZ if s == 0 else d)), None
                if s > 1 or (s == 1 and (m == 0) == (link == "zu")):
                    dep.append(f"{tag}{m}{link}{s - 1}")
                    before = add_to(ref(d), bufs[link](s - 1))
                p.send(f"{tag}{m}{link}{s}", link, ref(d), bufs[link](s), bufs[link](s), size, dep, None, before)
        return [f"{tag}{m}{link}{HZ - 1}" for link in ("zu", "zd")]

    def add2(ref, b1, b2):
        def fn():
            ref[...] += b1[...] + b2[...]

        return fn

    for m in range(2):
        bufs = {
            "zu": lambda s, m=m: rbu.at[s, ms[m]],
            "zd": lambda s, m=m: rbd.at[s, ms[m]],
        }
        fin = reduce_ring("B", lambda d, m=m: gB(d, 0, m), bufs, KB, m, lambda d, m=m: [f"rx{m}{d}"])
        p.step(f"finB{m}", 0.05, add2(gB(0, 0, m), bufs["zu"](HZ - 1), bufs["zd"](HZ - 1)), fin + [f"rx{m}0"])
    for m in range(2):
        for a in (1, 0):
            bufs = {
                "zu": lambda s, m=m, a=a: rau.at[s, js[a], ms[m]],
                "zd": lambda s, m=m, a=a: rad.at[s, js[a], ms[m]],
            }
            tag = "AO"[a]
            fin = reduce_ring(tag, lambda d, m=m, a=a: gA(d, a, m), bufs, KA, m, lambda d: ["gA"])
            p.step(f"fin{tag}{m}", 0.05, add2(gA(0, a, m), bufs["zu"](HZ - 1), bufs["zd"](HZ - 1)), fin)
        buf = rax.at[ms[m]]
        p.send(f"rax{m}", "in", gA(0, 1, m), buf, buf, KA, [f"finO{m}"])
        p.step(f"sumA{m}", 0.05, add_to(gA(0, 0, m), buf), [f"rax{m}", f"finA{m}"])
    p.send("cB", "cross", g.at[z, j, 1 - hf, :, B], rc.at[:, B], rc.at[:, B], KB, ["finB1"])
    p.send("cA", "cross", g.at[z, j, 1 - hf, :, A], rc.at[:, A], rc.at[:, A], KA, ["sumA1"])

    def own_out():
        for m, out in enumerate((gu_out, gd_out)):
            out[pl.ds(NF * hf, NF)] = g[z, j, hf, m]

    def other_out():
        for m, out in enumerate((gu_out, gd_out)):
            out[pl.ds(oh, NF)] = rc[m]

    p.step("own_out", 0.1, own_out, ["finB0", "sumA0"])
    p.step("other_out", 0.1, other_out, ["cA", "cB"])
    p.run()


def finish(ig, gu, gd, mu, md, ig_out, mu_out, md_out):
    ig_out[...] = ig[...]
    mu_out[...] = 0.9 * mu[...] + (1.0 / 64.0) * gu[...]
    md_out[...] = 0.9 * md[...] + (1.0 / 64.0) * gd[...]


def shards(inputs, cotangent, up_blocks, down_blocks, up_index, down_index, mom_up, mom_down):
    f, kb, r, b = up_blocks.shape
    tiles = lambda a: a.reshape(f, kb // 2, 2 * r, b)
    rows8 = lambda a: a.reshape(16, 8, 32, b).transpose(0, 2, 1, 3)
    vm = lambda *s: pltpu.VMEM(s, F32)
    hbm, smem = pl.BlockSpec(memory_space=pl.ANY), pl.BlockSpec(memory_space=pltpu.SMEM)
    vmem = pl.BlockSpec(memory_space=pltpu.VMEM)
    tile = (2, 8, 128)
    out_shape = (
        jax.ShapeDtypeStruct((128, 512), F32),
        jax.ShapeDtypeStruct((f, *tile), F32),
        jax.ShapeDtypeStruct((f, *tile), F32),
    )
    ig, gu, gd = pl.pallas_call(
        kernel,
        out_shape=out_shape,
        in_specs=[smem] * 2 + [hbm] * 4,
        out_specs=(vmem, vmem, vmem),
        scratch_shapes=[
            vm(2, 16, 32, 8, 128),
            vm(2, 16, 32, 8, 128),
            vm(NZ, 2, 2, 2, NF, *tile),
            vm(NZ, 2, 2, 2, NF, *tile),
            vm(NF, 256, 128),
            vm(NF, 256, 128),
            vm(4 * NF + 1, 256, 128),
            vm(NY, 2, 4, 256, 128),
            vm(NZ // 2, 2, 2, 2, NA, *tile),
            vm(NZ // 2, 2, 2, 2, NA, *tile),
            vm(NZ // 2, 2, 2, NF - NA, *tile),
            vm(NZ // 2, 2, 2, NF - NA, *tile),
            vm(NZ, 2, 2, NF - NA, *tile),
            vm(2, 2, NA, *tile),
            vm(2, NF, *tile),
            vm(NY, 4, 256, 128),
            vm(2, 4, 256, 128),
            vm(2, 4, 256, 128),
            vm(4, 128, 128),
            pltpu.SMEM((NF, 32), jnp.int32),
            pltpu.SemaphoreType.DMA((4,)),
            pltpu.SemaphoreType.DMA((256,)),
            pltpu.SemaphoreType.DMA((256,)),
        ],
        compiler_params=pltpu.CompilerParams(
            collective_id=0, has_side_effects=True, vmem_limit_bytes=60 * 1024 * 1024
        ),
    )(up_index.T, down_index.T, rows8(inputs), rows8(cotangent), tiles(up_blocks), tiles(down_blocks))
    ig, mu, md = pl.pallas_call(finish, out_shape=out_shape, in_specs=[vmem] * 5, out_specs=(vmem,) * 3)(
        ig, gu, gd, tiles(mom_up), tiles(mom_down)
    )
    return ig, mu.reshape(mom_up.shape), md.reshape(mom_down.shape)


def solution(mesh):
    return jax.shard_map(
        shards,
        mesh=mesh,
        in_specs=(
            P("tok", None),
            P("tok", None),
            P("hid", None, "tok", None),
            P("hid", None, "tok", None),
            P("hid", None),
            P("hid", None),
            P("hid", None, "tok", None),
            P("hid", None, "tok", None),
        ),
        out_specs=(P("tok", "hid"), P("hid", None, "tok", None), P("hid", None, "tok", None)),
        check_vma=False,
    )
```

```python
import functools
import heapq

import jax
import jax.numpy as jnp
from jax import lax
from jax.experimental import pallas as pl
from jax.experimental.pallas import tpu as pltpu
from jax.sharding import PartitionSpec as P

MESH = pl.DeviceIdType.MESH
NX, NY, NZ = 4, 4, 8
NF = 7
CHUNKS = (((0, 2), (2, 2)), ((4, 1), (5, 2)))
NSEND, NRECV = 47, 113
DEPTH = 3.0
BF, F32 = jnp.bfloat16, jnp.float32


def split(a):
    hi = a.astype(BF)
    return hi, (a - hi.astype(F32)).astype(BF)


def dot3(a, b, dims):
    ah, al = a
    bh, bl = b
    d = functools.partial(lax.dot_general, dimension_numbers=(dims, ((), ())), preferred_element_type=F32)
    return d(ah, bh) + d(ah, bl) + d(al, bh)


def merge4(lo, a, b):
    ra, rb = pltpu.roll(a, 4, 1), pltpu.roll(b, 4, 1)
    return jnp.where(lo, a, rb), jnp.where(lo, ra, b)


class Plan:
    RATE = {"core": 500.0}
    LAT = {"core": 1.0, "cross": 1.9, "in": 1.9, "yu": 1.9, "yd": 1.9, "zu": 2.2, "zd": 2.2}

    def __init__(self, ssem, rsem, devs):
        self.ssem, self.rsem, self.devs = ssem, rsem, devs
        self.items = []

    def send(self, name, link, src, dst, arrive, size, deps=(), land=None, before=None, rank=0):
        self.items.append(
            dict(name=name, link=link, src=src, dst=dst, arrive=arrive, size=size, deps=set(deps), land=land, before=before, rank=rank)
        )

    def step(self, name, cost, fn, deps=(), rank=0):
        self.items.append(dict(name=name, link=None, cost=cost, fn=fn, deps=set(deps), rank=rank))

    def order(self):
        now, free, done, flying, tick, ops = 0.0, {}, set(), [], 0, []
        todo = sorted(self.items, key=lambda i: i["rank"])
        while todo or flying:
            for it in [i for i in todo if i["link"] and i["deps"] <= done]:
                if free.get(it["link"], 0.0) - now > DEPTH:
                    continue
                todo.remove(it)
                end = max(now, free.get(it["link"], 0.0)) + it["size"] / 1e3 / self.RATE.get(it["link"], 46.0)
                free[it["link"]] = it["end"] = end
                it["start"] = now
                ops.append(("send", it))
                heapq.heappush(flying, (end + self.LAT[it["link"]], tick, it))
                tick += 1
            ready = next((i for i in todo if not i["link"] and i["deps"] <= done), None)
            if ready is not None and not (flying and flying[0][0] <= now):
                todo.remove(ready)
                ops.append(("step", ready))
                now += ready["cost"]
                done.add(ready["name"])
                continue
            when, _, it = heapq.heappop(flying)
            now = max(now, when)
            ops.append(("recv", it))
            done.add(it["name"])
        return ops

    def semaphores(self, ops):
        back = {"zu": "zd", "zd": "zu", "yu": "yd", "yd": "yu"}
        sent_at = {id(it): n for n, (what, it) in enumerate(ops) if what == "send"}
        got_at = {id(it): n for n, (what, it) in enumerate(ops) if what == "recv"}
        nsend, nrecv, sends, recvs = 0, 0, [], {}
        for n, (what, it) in enumerate(ops):
            if what != "send":
                continue
            it["after"] = None
            old = next((o for o in sends if o["end"] + 2.0 < it["start"]), None)
            if old is None:
                it["ssem"] = nsend
                nsend += 1
            else:
                it["ssem"], it["after"] = old["ssem"], old
                sends.remove(old)
            sends.append(it)
            link = it["link"]
            echo = [sent_at[id(o)] for w2, o in ops[:n] if w2 == "recv" and o["link"] == back.get(link, link)]
            last = max(echo, default=-1)
            pool = recvs.setdefault(link, [])
            old = next((o for o in pool if got_at[id(o)] < last), None)
            if old is None:
                it["rsem"] = nrecv
                nrecv += 1
            else:
                it["rsem"] = old["rsem"]
                pool.remove(old)
            pool.append(it)
        return sends, nsend, nrecv

    def run(self):
        ops = self.order()
        rest, nsend, nrecv = self.semaphores(ops)
        assert nsend <= NSEND and nrecv <= NRECV, (nsend, nrecv)
        for what, it in ops:
            if what == "step":
                it["fn"]()
            elif what == "recv":
                it["wait"].wait_recv()
                if it["land"] is not None:
                    it["land"]()
            else:
                if it["before"] is not None:
                    it["before"]()
                if it["after"] is not None:
                    it["after"]["copy"].wait_send()
                it["copy"], it["wait"] = (
                    pltpu.make_async_remote_copy(
                        s, d, self.ssem.at[it["ssem"]], self.rsem.at[it["rsem"]],
                        device_id=self.devs[it["link"]], device_id_type=MESH,
                    )
                    for s, d in ((it["src"], it["dst"]), (it["arrive"], it["arrive"]))
                )
                it["copy"].start()
        for it in rest:
            it["copy"].wait_send()


def kernel(
    ui, di, x_h, c_h, up_h, dn_h,
    ig_out, gu_out, gd_out,
    xo, xp, w, g, act, gpre, terms, ig,
    rau, rad, rbu, rbd, rx, rax, rc, cs, ryu, ryd, rp, slot,
    lsem, ssem, rsem,
):
    t, h = lax.axis_index("tok"), lax.axis_index("hid")
    z, x = t // NX, lax.rem(t, NX)
    y, c = h // 2, lax.rem(h, 2)
    hf = x // 2
    j = jnp.where((x == 1) | (x == 2), 1, 0)
    zz = lambda d: lax.rem(z + d + NZ, NZ)
    yy = lambda d: lax.rem(y + d + NY, NY)
    tok = lambda tz, tx: tz * NX + tx
    devs = {
        "cross": (tok(z, 3 - x), h),
        "in": (tok(z, x + 1 - 2 * lax.rem(x, 2)), h),
        "zu": (tok(zz(1), x), h),
        "zd": (tok(zz(-1), x), h),
        "yu": (t, yy(1) * 2 + c),
        "yd": (t, yy(-1) * 2 + c),
        "core": (t, y * 2 + 1 - c),
    }
    barrier = pltpu.get_barrier_semaphore()
    for dev in devs.values():
        pl.semaphore_signal(barrier, inc=1, device_id=dev, device_id_type=MESH)

    def local(n, src, dst):
        cp = pltpu.make_async_copy(src, dst, lsem.at[n])
        cp.start()
        return cp

    lw = [
        local(0, up_h.at[pl.ds(NF * hf, NF)], w.at[z, j, hf, 0]),
        local(1, dn_h.at[pl.ds(NF * hf, NF)], w.at[z, j, hf, 1]),
    ]
    lx = [local(2, x_h, xo.at[0]), local(3, c_h, xo.at[1])]
    for cp in lw:
        cp.wait()
    pl.semaphore_wait(barrier, len(devs))

    p = Plan(ssem, rsem, devs)
    HZ = NZ // 2
    js, ms = (j, 1 - j), (hf, 1 - hf)
    oh = NF * (1 - hf)
    KF = 2 * 8192

    def weight_gather(q, rank):
        (a0, an), (b0, bn) = CHUNKS[q]
        A, B = pl.ds(a0, an), pl.ds(b0, bn)
        wA = lambda d, a, m: w.at[zz(d), js[a], ms[m], :, A]
        wB = lambda d, a, m: w.at[zz(d), js[a], ms[m], :, B]
        need = []

        def ring(tag, ref, size, m, deps0):
            have = {0: deps0}
            for s in range(HZ):
                for link, sg in (("zu", -1), ("zd", 1)):
                    if s == HZ - 1 and (m == 0) != (link == "zu"):
                        continue
                    name = f"g{q}{tag}{m}{link}{s}"
                    p.send(name, link, ref(sg * s), ref(sg * s), ref(sg * (s + 1)), size, have[sg * s], rank=rank)
                    have[HZ if s == HZ - 1 else sg * (s + 1)] = [name]
                    need.append(name)
            return have

        for m in range(2):
            w0a, w0b = ([], []) if m == 0 else ([f"w{q}a0", f"w{q}a1"], [f"w{q}b0", f"w{q}b1"])
            p.send(f"ax{q}{m}", "in", wA(0, 0, m), wA(0, 0, m), wA(0, 1, m), an * KF, w0a, rank=rank)
            need.append(f"ax{q}{m}")
            hb = ring("b", lambda d, m=m: wB(d, 0, m), bn * KF, m, w0b)
            for d in (0, -1, 1, -2, 2, -3, 3, HZ):
                p.send(f"bx{q}{m}{d}", "in", wB(d, 0, m), wB(d, 0, m), wB(d, 1, m), bn * KF, hb[d], rank=rank)
                need.append(f"bx{q}{m}{d}")
            ring("a", lambda d, m=m: wA(d, 0, m), an * KF, m, w0a)
            ring("o", lambda d, m=m: wA(d, 1, m), an * KF, m, [f"ax{q}{m}"])
            if m == 0:
                for tag, F, lo_f, n_f in (("b", B, b0, bn), ("a", A, a0, an)):
                    for e, ref in enumerate((up_h, dn_h)):
                        p.send(
                            f"w{q}{tag}{e}", "cross", ref.at[pl.ds(oh + lo_f, n_f)],
                            w.at[z, j, hf, e, F], w.at[z, j, 1 - hf, e, F], n_f * 8192, rank=rank,
                        )
        return need

    need_w = [weight_gather(0, 0), weight_gather(1, 2)]

    RH = 4
    need_t = []
    KT = RH * 8 * 512 * 4

    def share(m, r, ty, tc, sub=None):
        rows = pl.ds(r * RH, RH) if sub is None else pl.ds(r * RH + sub * (RH // 2), RH // 2)
        return xp.at[m, rows, pl.ds((tc * NY + ty) * 4, 4)]

    for m in range(2):
        for r in range(16 // RH):
            k = f"{m}{r}"
            sh = lambda d, q=c, sub=None, m=m, r=r: share(m, r, yy(d), q, sub)
            src = (x_h, c_h)[m].at[pl.ds(r * RH, RH), pl.ds((c * NY + y) * 4, 4)]
            p.send(f"t{k}", "cross", src, sh(0), sh(0), KT, rank=1 if r + 4 * m < 4 else 3)
            p.send(f"tyu{k}", "yu", sh(0), sh(0), sh(-1), KT, [f"t{k}"])
            p.send(f"tyd{k}", "yd", sh(0), sh(0), sh(1), KT, [f"t{k}"])
            p.send(f"tzu{k}", "yu", sh(-1, c, 0), sh(-1, c, 0), sh(-2, c, 0), KT // 2, [f"tyu{k}"])
            p.send(f"tzd{k}", "yd", sh(1, c, 1), sh(1, c, 1), sh(2, c, 1), KT // 2, [f"tyd{k}"])
            for d, dep in ((0, [f"t{k}"]), (-1, [f"tyu{k}"]), (1, [f"tyd{k}"]), (2, [f"tzu{k}", f"tzd{k}"])):
                p.send(f"tc{k}{d}", "core", sh(d), sh(d), sh(d, 1 - c), KT, dep)
                need_t.append(f"tc{k}{d}")

    def make_slots():
        for i in range(NF):
            picks = [ui[k, NF * hf + i] for k in range(4)]

            def one(b, carry, i=i, picks=picks):
                v = jnp.int32(4 * NF)
                for k in range(4):
                    v = jnp.where(picks[k] == b, 4 * i + k, v)
                slot[i, b] = v
                return carry

            lax.fori_loop(0, 32, one, 0)
        terms[4 * NF] = jnp.zeros((256, 128), F32)

    p.step("slots", 0.5, make_slots)
    lo = lax.broadcasted_iota(jnp.int32, (NZ, 8, 128), 1) < 4

    def weights(m, i):
        out = []
        for kp in range(2):
            x0, x3, x1, x2 = (w[:, jj, mm, m, i, kp] for jj in range(2) for mm in range(2))
            a0, b0 = merge4(lo, x0, x1)
            a1, b1 = merge4(lo, x2, x3)
            out += [jnp.stack([a0, a1], 1).reshape(128, 128), jnp.stack([b0, b1], 1).reshape(128, 128)]
        return out

    def tokens(m, idx, i):
        cols = []
        for k in range(4):
            b = idx[k, NF * hf + i]
            cols.append(jnp.concatenate([xo[m, :, b].reshape(128, 128), xp[m, :, b].reshape(128, 128)], 0))
        return split(jnp.concatenate(cols, 1))

    def forward(i, carry):
        wu = split(jnp.concatenate(weights(0, i), 0))
        wd = split(jnp.concatenate(weights(1, i), 1))
        pre = dot3(tokens(0, ui, i), wu, ((1,), (0,)))
        ga = dot3(tokens(1, di, i), wd, ((1,), (1,)))
        sg = 1.0 / (1.0 + jnp.exp(-pre))
        act[i] = pre * sg
        gp = ga * sg * (1.0 + pre * (1.0 - sg))
        gpre[i] = gp
        back = dot3(split(gp), wu, ((1,), (1,)))
        for k in range(4):
            terms[i * 4 + k] = back[:, k * 128 : (k + 1) * 128]
        return carry

    def gather_terms(b, carry):
        total = terms[slot[0, b]]
        for i in range(1, NF):
            total = total + terms[slot[i, b]]
        ig[b // 8, lax.rem(b // 4, 2), lax.rem(b, 4)] = total
        return carry

    def grads(i, carry):
        gp = split(gpre[i])
        ac = split(act[i])
        gu = dot3(tokens(0, ui, i), gp, ((0,), (0,)))
        gd = dot3(ac, tokens(1, di, i), ((0,), (0,)))
        for m, full in enumerate((gu, gd)):
            for kp in range(2):
                if m == 0:
                    k0, k1 = (full[(2 * kp + e) * 128 : (2 * kp + e + 1) * 128] for e in range(2))
                else:
                    k0, k1 = (full[:, (2 * kp + e) * 128 : (2 * kp + e + 1) * 128] for e in range(2))
                k0, k1 = k0.reshape(NZ, 2, 8, 128), k1.reshape(NZ, 2, 8, 128)
                x0, x1 = merge4(lo, k0[:, 0], k1[:, 0])
                x2, x3 = merge4(lo, k0[:, 1], k1[:, 1])
                g[:, 0, 0, m, i, kp] = x0
                g[:, 1, 0, m, i, kp] = x1
                g[:, 1, 1, m, i, kp] = x2
                g[:, 0, 1, m, i, kp] = x3
        return carry

    loop = lambda a, b, fn: lambda: lax.fori_loop(a, b, fn, 0) and None

    def wait_own():
        for cp in lx:
            cp.wait()

    p.step("own", 0.1, wait_own)
    chunk_fs = [[f for f0, n in ch for f in range(f0, f0 + n)] for ch in CHUNKS]
    for q, fs in enumerate(chunk_fs):
        for i in fs:
            p.step(f"fwd{i}", 1.3, loop(i, i + 1, forward), need_w[q] + need_t + ["own", "slots"], rank=10 + 2 * q)
        p.step(f"grad{q}", 0.55 * len(fs), [loop(f0, f0 + n, grads) for f0, n in ((fs[0], len(fs)),)][0],
               [f"fwd{i}" for i in fs] + (["terms"] if q else []), rank=11 + 3 * q)
    p.step("terms", 0.5, loop(0, 32, gather_terms), [f"fwd{i}" for i in range(NF)], rank=13)

    KI = 256 * 128 * 4

    def add_ig(d, b, buf):
        def fn():
            ig[yy(d), c, b] += buf[...]

        return fn

    for n, d in enumerate((2, 1, -1, 0)):
        for b in range(4):
            buf = cs.at[n, b]
            p.send(f"c{d}{b}", "core", ig.at[yy(d), 1 - c, b], buf, buf, KI, ["terms"], add_ig(d, b, buf), rank=20 + b % 2)
    for b in range(4):
        for link, sg, buf in (("yu", 1, ryu), ("yd", -1, ryd)):
            dep, before = [f"c{sg}{b}"], None
            if (b < 2) == (link == "yu"):
                p.send(f"y2{b}", link, ig.at[yy(2), c, b], buf.at[0, b], buf.at[0, b], KI, [f"c2{b}"], rank=20 + b % 2)
                dep.append(f"y2{b}")
                before = add_ig(sg, b, buf.at[0, b])
            p.send(f"y1{link}{b}", link, ig.at[yy(sg), c, b], buf.at[1, b], buf.at[1, b], KI, dep, None, before, rank=20 + b % 2)

    def ig_sum(b):
        def fn():
            ig[y, c, b] += ryu[1, b] + ryd[1, b]

        return fn

    def ig_final(b):
        def fn():
            ig_out[:, b * 128 : (b + 1) * 128] = ig[y, c, b, 0:128] + rp[b]

        return fn

    for b in range(4):
        p.send(
            f"p{b}", "cross", ig.at[y, c, b, pl.ds(128, 128)], rp.at[b], rp.at[b], KI // 2,
            [f"y1yu{b}", f"y1yd{b}", f"c0{b}"], ig_final(b), ig_sum(b), rank=20,
        )

    zorder = (HZ, 3, -3, 2, -2, 1, -1, 0)

    def add_to(ref, buf):
        def fn():
            ref[...] += buf[...]

        return fn

    def add2(ref, b1, b2):
        def fn():
            ref[...] += b1[...] + b2[...]

        return fn

    def weight_reduce(q, rank):
        (a0, an), (b0, bn) = CHUNKS[q]
        A, B = pl.ds(a0, an), pl.ds(b0, bn)
        ready = [f"grad{q}"]
        gA = lambda d, a, m: g.at[zz(d), js[a], ms[m], :, A]
        gB = lambda d, a, m: g.at[zz(d), js[a], ms[m], :, B]
        for n, d in enumerate(zorder):
            for m in range(2):
                buf = rx.at[n, ms[m], :, B]
                p.send(f"rx{q}{m}{d}", "in", gB(d, 1, m), buf, buf, bn * KF, ready, add_to(gB(d, 0, m), buf), rank=rank)

        def ring(tag, ref, bufs, size, m, deps):
            for s in range(HZ):
                for link, sg in (("zu", 1), ("zd", -1)):
                    if s == 0 and (m == 0) != (link == "zu"):
                        continue
                    d = sg * (HZ - s)
                    dep, before = list(deps(HZ if s == 0 else d)), None
                    if s > 1 or (s == 1 and (m == 0) == (link == "zu")):
                        dep.append(f"r{q}{tag}{m}{link}{s - 1}")
                        before = add_to(ref(d), bufs[link](s - 1))
                    p.send(f"r{q}{tag}{m}{link}{s}", link, ref(d), bufs[link](s), bufs[link](s), size, dep, None, before, rank=rank)
            return [f"r{q}{tag}{m}{link}{HZ - 1}" for link in ("zu", "zd")]

        for m in range(2):
            bufs = {
                "zu": lambda s, m=m: rbu.at[s, ms[m], :, B],
                "zd": lambda s, m=m: rbd.at[s, ms[m], :, B],
            }
            fin = ring("B", lambda d, m=m: gB(d, 0, m), bufs, bn * KF, m, lambda d, m=m: [f"rx{q}{m}{d}"])
            p.step(f"finB{q}{m}", 0.05, add2(gB(0, 0, m), bufs["zu"](HZ - 1), bufs["zd"](HZ - 1)), fin + [f"rx{q}{m}0"])
        for m in range(2):
            for a in (1, 0):
                bufs = {
                    "zu": lambda s, m=m, a=a: rau.at[s, js[a], ms[m], :, A],
                    "zd": lambda s, m=m, a=a: rad.at[s, js[a], ms[m], :, A],
                }
                tag = "AO"[a]
                fin = ring(tag, lambda d, m=m, a=a: gA(d, a, m), bufs, an * KF, m, lambda d: ready)
                p.step(f"fin{tag}{q}{m}", 0.05, add2(gA(0, a, m), bufs["zu"](HZ - 1), bufs["zd"](HZ - 1)), fin)
            buf = rax.at[ms[m], :, A]
            p.send(f"rax{q}{m}", "in", gA(0, 1, m), buf, buf, an * KF, [f"finO{q}{m}"], rank=rank - 1)
            p.step(f"sumA{q}{m}", 0.05, add_to(gA(0, 0, m), buf), [f"rax{q}{m}", f"finA{q}{m}"])
        p.send(f"cB{q}", "cross", g.at[z, j, 1 - hf, :, B], rc.at[:, B], rc.at[:, B], bn * KF, [f"finB{q}1"], rank=rank)
        p.send(f"cA{q}", "cross", g.at[z, j, 1 - hf, :, A], rc.at[:, A], rc.at[:, A], an * KF, [f"sumA{q}1"], rank=rank)
        return [f"finB{q}0", f"sumA{q}0"], [f"cB{q}", f"cA{q}"]

    outs = [weight_reduce(0, 30), weight_reduce(1, 32)]

    def own_out():
        for m, out in enumerate((gu_out, gd_out)):
            out[pl.ds(NF * hf, NF)] = g[z, j, hf, m]

    def other_out():
        for m, out in enumerate((gu_out, gd_out)):
            out[pl.ds(oh, NF)] = rc[m]

    p.step("own_out", 0.1, own_out, outs[0][0] + outs[1][0])
    p.step("other_out", 0.1, other_out, outs[0][1] + outs[1][1])
    p.run()


def finish(ig, gu, gd, mu, md, ig_out, mu_out, md_out):
    ig_out[...] = ig[...]
    mu_out[...] = 0.9 * mu[...] + (1.0 / 64.0) * gu[...]
    md_out[...] = 0.9 * md[...] + (1.0 / 64.0) * gd[...]


def shards(inputs, cotangent, up_blocks, down_blocks, up_index, down_index, mom_up, mom_down):
    f, kb, r, b = up_blocks.shape
    tiles = lambda a: a.reshape(f, kb // 2, 2 * r, b)
    rows8 = lambda a: a.reshape(16, 8, 32, b).transpose(0, 2, 1, 3)
    vm = lambda *s: pltpu.VMEM(s, F32)
    hbm, smem = pl.BlockSpec(memory_space=pl.ANY), pl.BlockSpec(memory_space=pltpu.SMEM)
    vmem = pl.BlockSpec(memory_space=pltpu.VMEM)
    tile = (2, 8, 128)
    out_shape = (
        jax.ShapeDtypeStruct((128, 512), F32),
        jax.ShapeDtypeStruct((f, *tile), F32),
        jax.ShapeDtypeStruct((f, *tile), F32),
    )
    ig, gu, gd = pl.pallas_call(
        kernel,
        out_shape=out_shape,
        in_specs=[smem] * 2 + [hbm] * 4,
        out_specs=(vmem, vmem, vmem),
        scratch_shapes=[
            vm(2, 16, 32, 8, 128),
            vm(2, 16, 32, 8, 128),
            vm(NZ, 2, 2, 2, NF, *tile),
            vm(NZ, 2, 2, 2, NF, *tile),
            vm(NF, 256, 128),
            vm(NF, 256, 128),
            vm(4 * NF + 1, 256, 128),
            vm(NY, 2, 4, 256, 128),
            vm(NZ // 2, 2, 2, 2, NF, *tile),
            vm(NZ // 2, 2, 2, 2, NF, *tile),
            vm(NZ // 2, 2, 2, NF, *tile),
            vm(NZ // 2, 2, 2, NF, *tile),
            vm(NZ, 2, 2, NF, *tile),
            vm(2, 2, NF, *tile),
            vm(2, NF, *tile),
            vm(NY, 4, 256, 128),
            vm(2, 4, 256, 128),
            vm(2, 4, 256, 128),
            vm(4, 128, 128),
            pltpu.SMEM((NF, 32), jnp.int32),
            pltpu.SemaphoreType.DMA((4,)),
            pltpu.SemaphoreType.DMA((NSEND,)),
            pltpu.SemaphoreType.DMA((NRECV,)),
        ],
        compiler_params=pltpu.CompilerParams(
            collective_id=0, has_side_effects=True, vmem_limit_bytes=60 * 1024 * 1024
        ),
    )(up_index.T, down_index.T, rows8(inputs), rows8(cotangent), tiles(up_blocks), tiles(down_blocks))
    ig, mu, md = pl.pallas_call(finish, out_shape=out_shape, in_specs=[vmem] * 5, out_specs=(vmem,) * 3)(
        ig, gu, gd, tiles(mom_up), tiles(mom_down)
    )
    return ig, mu.reshape(mom_up.shape), md.reshape(mom_down.shape)


def solution(mesh):
    return jax.shard_map(
        shards,
        mesh=mesh,
        in_specs=(
            P("tok", None),
            P("tok", None),
            P("hid", None, "tok", None),
            P("hid", None, "tok", None),
            P("hid", None),
            P("hid", None),
            P("hid", None, "tok", None),
            P("hid", None, "tok", None),
        ),
        out_specs=(P("tok", "hid"), P("hid", None, "tok", None), P("hid", None, "tok", None)),
        check_vma=False,
    )
```

```python
import functools
import heapq

import jax
import jax.numpy as jnp
from jax import lax
from jax.experimental import pallas as pl
from jax.experimental.pallas import tpu as pltpu
from jax.sharding import PartitionSpec as P

MESH = pl.DeviceIdType.MESH
NX, NY, NZ = 4, 4, 8
NF = 7
CHUNKS = (((0, 2), (2, 2)), ((4, 1), (5, 2)))
NSEND, NRECV = 38, 94
DEPTH = 1.5
BF, F32 = jnp.bfloat16, jnp.float32


def split(a):
    hi = a.astype(BF)
    return hi, (a - hi.astype(F32)).astype(BF)


def dot(a, b, dims):
    return lax.dot_general(a, b, (dims, ((), ())), preferred_element_type=F32)


def fold(a):
    return a[:, :128] + a[:, 128:]


def merge4(lo, a, b):
    ra, rb = pltpu.roll(a, 4, 1), pltpu.roll(b, 4, 1)
    return jnp.where(lo, a, rb), jnp.where(lo, ra, b)


class Plan:
    RATE = {"core": 500.0}
    LAT = {"core": 1.0, "cross": 1.9, "in": 1.9, "yu": 1.9, "yd": 1.9, "zu": 2.2, "zd": 2.2}

    def __init__(self, ssem, rsem, devs):
        self.ssem, self.rsem, self.devs = ssem, rsem, devs
        self.items = []

    def send(self, name, link, src, dst, arrive, size, deps=(), land=None, before=None, rank=0):
        self.items.append(
            dict(name=name, link=link, src=src, dst=dst, arrive=arrive, size=size, deps=set(deps), land=land, before=before, rank=rank)
        )

    def step(self, name, cost, fn, deps=(), rank=0):
        self.items.append(dict(name=name, link=None, cost=cost, fn=fn, deps=set(deps), rank=rank))

    def order(self):
        now, free, done, flying, tick, ops = 0.0, {}, set(), [], 0, []
        todo = sorted(self.items, key=lambda i: i["rank"])
        while todo or flying:
            for it in [i for i in todo if i["link"] and i["deps"] <= done]:
                if free.get(it["link"], 0.0) - now > DEPTH:
                    continue
                todo.remove(it)
                end = max(now, free.get(it["link"], 0.0)) + it["size"] / 1e3 / self.RATE.get(it["link"], 46.0)
                free[it["link"]] = it["end"] = end
                it["start"] = now
                ops.append(("send", it))
                heapq.heappush(flying, (end + self.LAT[it["link"]], tick, it))
                tick += 1
            ready = next((i for i in todo if not i["link"] and i["deps"] <= done), None)
            if ready is not None and not (flying and flying[0][0] <= now):
                todo.remove(ready)
                ops.append(("step", ready))
                now += ready["cost"]
                done.add(ready["name"])
                continue
            when, _, it = heapq.heappop(flying)
            now = max(now, when)
            ops.append(("recv", it))
            done.add(it["name"])
        return ops

    def semaphores(self, ops):
        back = {"zu": "zd", "zd": "zu", "yu": "yd", "yd": "yu"}
        sent_at = {id(it): n for n, (what, it) in enumerate(ops) if what == "send"}
        got_at = {id(it): n for n, (what, it) in enumerate(ops) if what == "recv"}
        nsend, nrecv, sends, recvs = 0, 0, [], {}
        for n, (what, it) in enumerate(ops):
            if what != "send":
                continue
            it["after"] = None
            old = next((o for o in sends if o["end"] + 2.0 < it["start"]), None)
            if old is None:
                it["ssem"] = nsend
                nsend += 1
            else:
                it["ssem"], it["after"] = old["ssem"], old
                sends.remove(old)
            sends.append(it)
            link = it["link"]
            echo = [sent_at[id(o)] for w2, o in ops[:n] if w2 == "recv" and o["link"] == back.get(link, link)]
            last = max(echo, default=-1)
            pool = recvs.setdefault(link, [])
            old = next((o for o in pool if got_at[id(o)] < last), None)
            if old is None:
                it["rsem"] = nrecv
                nrecv += 1
            else:
                it["rsem"] = old["rsem"]
                pool.remove(old)
            pool.append(it)
        return sends, nsend, nrecv

    def run(self):
        ops = self.order()
        rest, nsend, nrecv = self.semaphores(ops)
        assert nsend <= NSEND and nrecv <= NRECV, (nsend, nrecv)
        for what, it in ops:
            if what == "step":
                it["fn"]()
            elif what == "recv":
                it["wait"].wait_recv()
                if it["land"] is not None:
                    it["land"]()
            else:
                if it["before"] is not None:
                    it["before"]()
                if it["after"] is not None:
                    it["after"]["copy"].wait_send()
                it["copy"], it["wait"] = (
                    pltpu.make_async_remote_copy(
                        s, d, self.ssem.at[it["ssem"]], self.rsem.at[it["rsem"]],
                        device_id=self.devs[it["link"]], device_id_type=MESH,
                    )
                    for s, d in ((it["src"], it["dst"]), (it["arrive"], it["arrive"]))
                )
                it["copy"].start()
        for it in rest:
            it["copy"].wait_send()


def kernel(
    ui, di, x_h, c_h, up_h, dn_h,
    ig_out, gu_out, gd_out,
    xo, xp0, xp1, w, g, act, gpre, terms, ig,
    rau, rad, rbu, rbd, rx, rax, rc, cs, ryu, ryd, rp, wuh, wul, slot,
    lsem, ssem, rsem,
):
    t, h = lax.axis_index("tok"), lax.axis_index("hid")
    z, x = t // NX, lax.rem(t, NX)
    y, c = h // 2, lax.rem(h, 2)
    hf = x // 2
    j = jnp.where((x == 1) | (x == 2), 1, 0)
    zz = lambda d: lax.rem(z + d + NZ, NZ)
    yy = lambda d: lax.rem(y + d + NY, NY)
    tok = lambda tz, tx: tz * NX + tx
    devs = {
        "cross": (tok(z, 3 - x), h),
        "in": (tok(z, x + 1 - 2 * lax.rem(x, 2)), h),
        "zu": (tok(zz(1), x), h),
        "zd": (tok(zz(-1), x), h),
        "yu": (t, yy(1) * 2 + c),
        "yd": (t, yy(-1) * 2 + c),
        "core": (t, y * 2 + 1 - c),
    }
    barrier = pltpu.get_barrier_semaphore()
    for dev in devs.values():
        pl.semaphore_signal(barrier, inc=1, device_id=dev, device_id_type=MESH)

    def local(n, src, dst):
        cp = pltpu.make_async_copy(src, dst, lsem.at[n])
        cp.start()
        return cp

    lw = [
        local(0, up_h.at[pl.ds(NF * hf, NF)], w.at[z, j, hf, 0]),
        local(1, dn_h.at[pl.ds(NF * hf, NF)], w.at[z, j, hf, 1]),
    ]
    lx = [local(2, x_h, xo.at[0]), local(3, c_h, xo.at[1])]
    for cp in lw:
        cp.wait()
    pl.semaphore_wait(barrier, len(devs))

    p = Plan(ssem, rsem, devs)
    HZ = NZ // 2
    js, ms = (j, 1 - j), (hf, 1 - hf)
    oh = NF * (1 - hf)
    KF = 2 * 8192

    def weight_gather(q, rank):
        (a0, an), (b0, bn) = CHUNKS[q]
        A, B = pl.ds(a0, an), pl.ds(b0, bn)
        wA = lambda d, a, m: w.at[zz(d), js[a], ms[m], :, A]
        wB = lambda d, a, m: w.at[zz(d), js[a], ms[m], :, B]
        need = []

        def ring(tag, ref, size, m, deps0, rank):
            have = {0: deps0}
            for s in range(HZ):
                for link, sg in (("zu", -1), ("zd", 1)):
                    if s == HZ - 1 and (m == 0) != (link == "zu"):
                        continue
                    name = f"g{q}{tag}{m}{link}{s}"
                    p.send(name, link, ref(sg * s), ref(sg * s), ref(sg * (s + 1)), size, have[sg * s], rank=rank)
                    have[HZ if s == HZ - 1 else sg * (s + 1)] = [name]
                    need.append(name)
            return have

        for m in range(2):
            w0a, w0b = ([], []) if m == 0 else ([f"w{q}a0", f"w{q}a1"], [f"w{q}b0", f"w{q}b1"])
            p.send(f"ax{q}{m}", "in", wA(0, 0, m), wA(0, 0, m), wA(0, 1, m), an * KF, w0a, rank=rank - 0.5)
            need.append(f"ax{q}{m}")
            hb = ring("b", lambda d, m=m: wB(d, 0, m), bn * KF, m, w0b, rank + 0.15 - 0.1 * m)
            for d in (0, -1, 1, -2, 2, -3, 3, HZ):
                p.send(f"bx{q}{m}{d}", "in", wB(d, 0, m), wB(d, 0, m), wB(d, 1, m), bn * KF, hb[d], rank=rank)
                need.append(f"bx{q}{m}{d}")
            ring("a", lambda d, m=m: wA(d, 0, m), an * KF, m, w0a, rank + 0.3 - 0.1 * m)
            ring("o", lambda d, m=m: wA(d, 1, m), an * KF, m, [f"ax{q}{m}"], rank + 0.1 - 0.1 * m)
            if m == 0:
                for tag, F, lo_f, n_f in (("b", B, b0, bn), ("a", A, a0, an)):
                    for e, ref in enumerate((up_h, dn_h)):
                        p.send(
                            f"w{q}{tag}{e}", "cross", ref.at[pl.ds(oh + lo_f, n_f)],
                            w.at[z, j, hf, e, F], w.at[z, j, 1 - hf, e, F], n_f * 8192, rank=rank - 0.1 * (tag == "a"),
                        )
        return need

    need_w = [weight_gather(0, 0), weight_gather(1, 2)]

    RH = 4
    need_t = [], []
    KT = RH * 8 * 512 * 4

    def share(m, r, ty, tc, sub=None):
        rows = pl.ds(r * RH, RH) if sub is None else pl.ds(r * RH + sub * (RH // 2), RH // 2)
        return (xp0, xp1)[m].at[rows, pl.ds((tc * NY + ty) * 4, 4)]

    for m in range(2):
        for r in range(16 // RH):
            k = f"{m}{r}"
            sh = lambda d, q=c, sub=None, m=m, r=r: share(m, r, yy(d), q, sub)
            src = (x_h, c_h)[m].at[pl.ds(r * RH, RH), pl.ds((c * NY + y) * 4, 4)]
            p.send(f"t{k}", "cross", src, sh(0), sh(0), KT, rank=1 if r + 4 * m < 4 else 3)
            p.send(f"tyu{k}", "yu", sh(0), sh(0), sh(-1), KT, [f"t{k}"])
            p.send(f"tyd{k}", "yd", sh(0), sh(0), sh(1), KT, [f"t{k}"])
            p.send(f"tzu{k}", "yu", sh(-1, c, 0), sh(-1, c, 0), sh(-2, c, 0), KT // 2, [f"tyu{k}"])
            p.send(f"tzd{k}", "yd", sh(1, c, 1), sh(1, c, 1), sh(2, c, 1), KT // 2, [f"tyd{k}"])
            for d, dep in ((0, [f"t{k}"]), (-1, [f"tyu{k}"]), (1, [f"tyd{k}"]), (2, [f"tzu{k}", f"tzd{k}"])):
                p.send(f"tc{k}{d}", "core", sh(d), sh(d), sh(d, 1 - c), KT, dep)
                need_t[m].append(f"tc{k}{d}")

    def make_slots():
        for i in range(NF):
            picks = [ui[k, NF * hf + i] for k in range(4)]

            def one(b, carry, i=i, picks=picks):
                v = jnp.int32(4 * NF)
                for k in range(4):
                    v = jnp.where(picks[k] == b, 4 * i + k, v)
                slot[i, b] = v
                return carry

            lax.fori_loop(0, 32, one, 0)
        terms[4 * NF] = jnp.zeros((256, 128), F32)

    p.step("slots", 0.5, make_slots)
    lo = lax.broadcasted_iota(jnp.int32, (NZ, 8, 128), 1) < 4

    def weights(m, i):
        out = []
        for kp in range(2):
            x0, x3, x1, x2 = (w[:, jj, mm, m, i, kp] for jj in range(2) for mm in range(2))
            a0, b0 = merge4(lo, x0, x1)
            a1, b1 = merge4(lo, x2, x3)
            out += [jnp.stack([a0, a1], 1).reshape(128, 128), jnp.stack([b0, b1], 1).reshape(128, 128)]
        return out

    def tokens(m, idx, i):
        cols = []
        for k in range(4):
            b = idx[k, NF * hf + i]
            cols.append(jnp.concatenate([xo[m, :, b].reshape(128, 128), (xp0, xp1)[m][:, b].reshape(128, 128)], 0))
        return split(jnp.concatenate(cols, 1))

    def before(i):
        wh, wl = split(jnp.concatenate(weights(0, i), 0))
        wuh[i], wul[i] = wh, wl
        xh, xl = tokens(0, ui, i)
        act[i] = fold(dot(xh, jnp.concatenate([wh, wl], 1), ((1,), (0,)))) + dot(xl, wh, ((1,), (0,)))

    def after(i):
        wh, wl = split(jnp.concatenate(weights(1, i), 1))
        ch, cl = tokens(1, di, i)
        ga = fold(dot(ch, jnp.concatenate([wh, wl], 0), ((1,), (1,)))) + dot(cl, wh, ((1,), (1,)))
        pre = act[i]
        sg = 1.0 / (1.0 + jnp.exp(-pre))
        act[i] = pre * sg
        gp = ga * sg * (1.0 + pre * (1.0 - sg))
        gpre[i] = gp
        gh, gl = split(gp)
        uh, ul = wuh[i], wul[i]
        back = dot(jnp.concatenate([gh, gl], 1), jnp.concatenate([uh, uh], 1), ((1,), (1,))) + dot(gh, ul, ((1,), (1,)))
        for k in range(4):
            terms[i * 4 + k] = back[:, k * 128 : (k + 1) * 128]

    def gather_terms(b, carry):
        total = terms[slot[0, b]]
        for i in range(1, NF):
            total = total + terms[slot[i, b]]
        ig[b // 8, lax.rem(b // 4, 2), lax.rem(b, 4)] = total
        return carry

    def grads(i, carry):
        gh, gl = split(gpre[i])
        ah, al = split(act[i])
        xh, xl = tokens(0, ui, i)
        ch, cl = tokens(1, di, i)
        d00 = ((0,), (0,))
        gu = fold(dot(xh, jnp.concatenate([gh, gl], 1), d00)) + dot(xl, gh, d00)
        gd = dot(ah, ch, d00) + dot(ah, cl, d00) + dot(al, ch, d00)
        for m, full in enumerate((gu, gd)):
            for kp in range(2):
                if m == 0:
                    k0, k1 = (full[(2 * kp + e) * 128 : (2 * kp + e + 1) * 128] for e in range(2))
                else:
                    k0, k1 = (full[:, (2 * kp + e) * 128 : (2 * kp + e + 1) * 128] for e in range(2))
                k0, k1 = k0.reshape(NZ, 2, 8, 128), k1.reshape(NZ, 2, 8, 128)
                x0, x1 = merge4(lo, k0[:, 0], k1[:, 0])
                x2, x3 = merge4(lo, k0[:, 1], k1[:, 1])
                g[:, 0, 0, m, i, kp] = x0
                g[:, 1, 0, m, i, kp] = x1
                g[:, 1, 1, m, i, kp] = x2
                g[:, 0, 1, m, i, kp] = x3
        return carry

    loop = lambda a, b, fn: lambda: lax.fori_loop(a, b, fn, 0) and None

    def wait_own():
        for cp in lx:
            cp.wait()

    p.step("own", 0.1, wait_own)
    chunk_fs = [[f for f0, n in ch for f in range(f0, f0 + n)] for ch in CHUNKS]
    for q, fs in enumerate(chunk_fs):
        for i in fs:
            p.step(f"pre{i}", 0.45, functools.partial(before, i), need_w[q] + need_t[0] + ["own", "slots"], rank=10 + 2 * q)
            p.step(f"fwd{i}", 0.75, functools.partial(after, i), [f"pre{i}"] + need_t[1], rank=10 + 2 * q)
        p.step(f"grad{q}", 0.5 * len(fs), [loop(f0, f0 + n, grads) for f0, n in ((fs[0], len(fs)),)][0],
               [f"fwd{i}" for i in fs] + (["terms"] if q else []), rank=11 + 3 * q)
    p.step("terms", 0.5, loop(0, 32, gather_terms), [f"fwd{i}" for i in range(NF)], rank=13)

    KI = 256 * 128 * 4

    def add_ig(d, b, buf):
        def fn():
            ig[yy(d), c, b] += buf[...]

        return fn

    for n, d in enumerate((2, 1, -1, 0)):
        for b in range(4):
            buf = cs.at[n, b]
            p.send(f"c{d}{b}", "core", ig.at[yy(d), 1 - c, b], buf, buf, KI, ["terms"], add_ig(d, b, buf), rank=20 + b % 2)
    for b in range(4):
        for link, sg, buf in (("yu", 1, ryu), ("yd", -1, ryd)):
            dep, before = [f"c{sg}{b}"], None
            if (b < 2) == (link == "yu"):
                p.send(f"y2{b}", link, ig.at[yy(2), c, b], buf.at[0, b], buf.at[0, b], KI, [f"c2{b}"], rank=20 + b % 2)
                dep.append(f"y2{b}")
                before = add_ig(sg, b, buf.at[0, b])
            p.send(f"y1{link}{b}", link, ig.at[yy(sg), c, b], buf.at[1, b], buf.at[1, b], KI, dep, None, before, rank=20 + b % 2)

    def ig_sum(b):
        def fn():
            ig[y, c, b] += ryu[1, b] + ryd[1, b]

        return fn

    def ig_final(b):
        def fn():
            ig_out[:, b * 128 : (b + 1) * 128] = ig[y, c, b, 0:128] + rp[b]

        return fn

    for b in range(4):
        p.send(
            f"p{b}", "cross", ig.at[y, c, b, pl.ds(128, 128)], rp.at[b], rp.at[b], KI // 2,
            [f"y1yu{b}", f"y1yd{b}", f"c0{b}"], ig_final(b), ig_sum(b), rank=20,
        )

    zorder = (HZ, 3, -3, 2, -2, 1, -1, 0)

    def add_to(ref, buf):
        def fn():
            ref[...] += buf[...]

        return fn

    def add2(ref, b1, b2):
        def fn():
            ref[...] += b1[...] + b2[...]

        return fn

    def weight_reduce(q, rank):
        (a0, an), (b0, bn) = CHUNKS[q]
        A, B = pl.ds(a0, an), pl.ds(b0, bn)
        ready = [f"grad{q}"]
        gA = lambda d, a, m: g.at[zz(d), js[a], ms[m], :, A]
        gB = lambda d, a, m: g.at[zz(d), js[a], ms[m], :, B]
        for n, d in enumerate(zorder):
            for m in range(2):
                buf = rx.at[n, ms[m], :, B]
                p.send(f"rx{q}{m}{d}", "in", gB(d, 1, m), buf, buf, bn * KF, ready, add_to(gB(d, 0, m), buf), rank=rank)

        def ring(tag, ref, bufs, size, m, deps, rank):
            for s in range(HZ):
                for link, sg in (("zu", 1), ("zd", -1)):
                    if s == 0 and (m == 0) != (link == "zu"):
                        continue
                    d = sg * (HZ - s)
                    dep, before = list(deps(HZ if s == 0 else d)), None
                    if s > 1 or (s == 1 and (m == 0) == (link == "zu")):
                        dep.append(f"r{q}{tag}{m}{link}{s - 1}")
                        before = add_to(ref(d), bufs[link](s - 1))
                    p.send(f"r{q}{tag}{m}{link}{s}", link, ref(d), bufs[link](s), bufs[link](s), size, dep, None, before, rank=rank)
            return [f"r{q}{tag}{m}{link}{HZ - 1}" for link in ("zu", "zd")]

        for m in range(2):
            bufs = {
                "zu": lambda s, m=m: rbu.at[s, ms[m], :, B],
                "zd": lambda s, m=m: rbd.at[s, ms[m], :, B],
            }
            fin = ring("B", lambda d, m=m: gB(d, 0, m), bufs, bn * KF, m, lambda d, m=m: [f"rx{q}{m}{d}"], rank)
            p.step(f"finB{q}{m}", 0.05, add2(gB(0, 0, m), bufs["zu"](HZ - 1), bufs["zd"](HZ - 1)), fin + [f"rx{q}{m}0"])
        for m in range(2):
            for a in (1, 0):
                bufs = {
                    "zu": lambda s, m=m, a=a: rau.at[s, js[a], ms[m], :, A],
                    "zd": lambda s, m=m, a=a: rad.at[s, js[a], ms[m], :, A],
                }
                tag = "AO"[a]
                fin = ring(tag, lambda d, m=m, a=a: gA(d, a, m), bufs, an * KF, m, lambda d: ready, rank + 5)
                p.step(f"fin{tag}{q}{m}", 0.05, add2(gA(0, a, m), bufs["zu"](HZ - 1), bufs["zd"](HZ - 1)), fin)
            buf = rax.at[ms[m], :, A]
            p.send(f"rax{q}{m}", "in", gA(0, 1, m), buf, buf, an * KF, [f"finO{q}{m}"], rank=rank - 1)
            p.step(f"sumA{q}{m}", 0.05, add_to(gA(0, 0, m), buf), [f"rax{q}{m}", f"finA{q}{m}"])
        p.send(f"cB{q}", "cross", g.at[z, j, 1 - hf, :, B], rc.at[:, B], rc.at[:, B], bn * KF, [f"finB{q}1"], rank=rank)
        p.send(f"cA{q}", "cross", g.at[z, j, 1 - hf, :, A], rc.at[:, A], rc.at[:, A], an * KF, [f"sumA{q}1"], rank=rank)
        return [f"finB{q}0", f"sumA{q}0"], [f"cB{q}", f"cA{q}"]

    outs = [weight_reduce(0, 30), weight_reduce(1, 32)]

    def own_out():
        for m, out in enumerate((gu_out, gd_out)):
            out[pl.ds(NF * hf, NF)] = g[z, j, hf, m]

    def other_out():
        for m, out in enumerate((gu_out, gd_out)):
            out[pl.ds(oh, NF)] = rc[m]

    p.step("own_out", 0.1, own_out, outs[0][0] + outs[1][0])
    p.step("other_out", 0.1, other_out, outs[0][1] + outs[1][1])
    p.run()


def finish(ig, gu, gd, mu, md, ig_out, mu_out, md_out):
    ig_out[...] = ig[...]
    mu_out[...] = 0.9 * mu[...] + (1.0 / 64.0) * gu[...]
    md_out[...] = 0.9 * md[...] + (1.0 / 64.0) * gd[...]


def shards(inputs, cotangent, up_blocks, down_blocks, up_index, down_index, mom_up, mom_down):
    f, kb, r, b = up_blocks.shape
    tiles = lambda a: a.reshape(f, kb // 2, 2 * r, b)
    rows8 = lambda a: a.reshape(16, 8, 32, b).transpose(0, 2, 1, 3)
    vm = lambda *s: pltpu.VMEM(s, F32)
    hbm, smem = pl.BlockSpec(memory_space=pl.ANY), pl.BlockSpec(memory_space=pltpu.SMEM)
    vmem = pl.BlockSpec(memory_space=pltpu.VMEM)
    tile = (2, 8, 128)
    out_shape = (
        jax.ShapeDtypeStruct((128, 512), F32),
        jax.ShapeDtypeStruct((f, *tile), F32),
        jax.ShapeDtypeStruct((f, *tile), F32),
    )
    ig, gu, gd = pl.pallas_call(
        kernel,
        out_shape=out_shape,
        in_specs=[smem] * 2 + [hbm] * 4,
        out_specs=(vmem, vmem, vmem),
        scratch_shapes=[
            vm(2, 16, 32, 8, 128),
            vm(16, 32, 8, 128),
            vm(16, 32, 8, 128),
            vm(NZ, 2, 2, 2, NF, *tile),
            vm(NZ, 2, 2, 2, NF, *tile),
            vm(NF, 256, 128),
            vm(NF, 256, 128),
            vm(4 * NF + 1, 256, 128),
            vm(NY, 2, 4, 256, 128),
            vm(NZ // 2, 2, 2, 2, NF, *tile),
            vm(NZ // 2, 2, 2, 2, NF, *tile),
            vm(NZ // 2, 2, 2, NF, *tile),
            vm(NZ // 2, 2, 2, NF, *tile),
            vm(NZ, 2, 2, NF, *tile),
            vm(2, 2, NF, *tile),
            vm(2, NF, *tile),
            vm(NY, 4, 256, 128),
            vm(2, 4, 256, 128),
            vm(2, 4, 256, 128),
            vm(4, 128, 128),
            pltpu.VMEM((NF, 512, 128), BF),
            pltpu.VMEM((NF, 512, 128), BF),
            pltpu.SMEM((NF, 32), jnp.int32),
            pltpu.SemaphoreType.DMA((4,)),
            pltpu.SemaphoreType.DMA((NSEND,)),
            pltpu.SemaphoreType.DMA((NRECV,)),
        ],
        compiler_params=pltpu.CompilerParams(
            collective_id=0, has_side_effects=True, vmem_limit_bytes=60 * 1024 * 1024
        ),
    )(up_index.T, down_index.T, rows8(inputs), rows8(cotangent), tiles(up_blocks), tiles(down_blocks))
    ig, mu, md = pl.pallas_call(finish, out_shape=out_shape, in_specs=[vmem] * 5, out_specs=(vmem,) * 3)(
        ig, gu, gd, tiles(mom_up), tiles(mom_down)
    )
    return ig, mu.reshape(mom_up.shape), md.reshape(mom_down.shape)


def solution(mesh):
    return jax.shard_map(
        shards,
        mesh=mesh,
        in_specs=(
            P("tok", None),
            P("tok", None),
            P("hid", None, "tok", None),
            P("hid", None, "tok", None),
            P("hid", None),
            P("hid", None),
            P("hid", None, "tok", None),
            P("hid", None, "tok", None),
        ),
        out_specs=(P("tok", "hid"), P("hid", None, "tok", None), P("hid", None, "tok", None)),
        check_vma=False,
    )
```

```python
import functools
import heapq

import jax
import jax.numpy as jnp
from jax import lax
from jax.experimental import pallas as pl
from jax.experimental.pallas import tpu as pltpu
from jax.sharding import PartitionSpec as P

MESH = pl.DeviceIdType.MESH
NX, NY, NZ = 4, 4, 8
NF = 7
CHUNKS = (((0, 2), (2, 2)), ((4, 1), (5, 2)))
NSEND, NRECV = 38, 94
DEPTH = 1.5
BF, F32 = jnp.bfloat16, jnp.float32


def split(a):
    hi = a.astype(BF)
    return hi, (a - hi.astype(F32)).astype(BF)


def dot(a, b, dims):
    return lax.dot_general(a, b, (dims, ((), ())), preferred_element_type=F32)


def fold(a):
    return a[:, :128] + a[:, 128:]


def merge4(lo, a, b):
    ra, rb = pltpu.roll(a, 4, 1), pltpu.roll(b, 4, 1)
    return jnp.where(lo, a, rb), jnp.where(lo, ra, b)


class Plan:
    RATE = {"core": 500.0}
    LAT = {"core": 1.0, "cross": 1.9, "in": 1.9, "yu": 1.9, "yd": 1.9, "zu": 2.2, "zd": 2.2}

    def __init__(self, ssem, rsem, devs):
        self.ssem, self.rsem, self.devs = ssem, rsem, devs
        self.items = []

    def send(self, name, link, src, dst, arrive, size, deps=(), land=None, before=None, rank=0):
        self.items.append(
            dict(name=name, link=link, src=src, dst=dst, arrive=arrive, size=size, deps=set(deps), land=land, before=before, rank=rank)
        )

    def step(self, name, cost, fn, deps=(), rank=0):
        self.items.append(dict(name=name, link=None, cost=cost, fn=fn, deps=set(deps), rank=rank))

    def order(self):
        now, free, done, flying, tick, ops = 0.0, {}, set(), [], 0, []
        todo = sorted(self.items, key=lambda i: i["rank"])
        while todo or flying:
            for it in [i for i in todo if i["link"] and i["deps"] <= done]:
                if free.get(it["link"], 0.0) - now > DEPTH:
                    continue
                todo.remove(it)
                end = max(now, free.get(it["link"], 0.0)) + it["size"] / 1e3 / self.RATE.get(it["link"], 46.0)
                free[it["link"]] = it["end"] = end
                it["start"] = now
                ops.append(("send", it))
                heapq.heappush(flying, (end + self.LAT[it["link"]], tick, it))
                tick += 1
            ready = next((i for i in todo if not i["link"] and i["deps"] <= done), None)
            if ready is not None and not (flying and flying[0][0] <= now):
                todo.remove(ready)
                ops.append(("step", ready))
                now += ready["cost"]
                done.add(ready["name"])
                continue
            when, _, it = heapq.heappop(flying)
            now = max(now, when)
            ops.append(("recv", it))
            done.add(it["name"])
        return ops

    def semaphores(self, ops):
        back = {"zu": "zd", "zd": "zu", "yu": "yd", "yd": "yu"}
        sent_at = {id(it): n for n, (what, it) in enumerate(ops) if what == "send"}
        got_at = {id(it): n for n, (what, it) in enumerate(ops) if what == "recv"}
        nsend, nrecv, sends, recvs = 0, 0, [], {}
        for n, (what, it) in enumerate(ops):
            if what != "send":
                continue
            it["after"] = None
            old = next((o for o in sends if o["end"] + 2.0 < it["start"]), None)
            if old is None:
                it["ssem"] = nsend
                nsend += 1
            else:
                it["ssem"], it["after"] = old["ssem"], old
                sends.remove(old)
            sends.append(it)
            link = it["link"]
            echo = [sent_at[id(o)] for w2, o in ops[:n] if w2 == "recv" and o["link"] == back.get(link, link)]
            last = max(echo, default=-1)
            pool = recvs.setdefault(link, [])
            old = next((o for o in pool if got_at[id(o)] < last), None)
            if old is None:
                it["rsem"] = nrecv
                nrecv += 1
            else:
                it["rsem"] = old["rsem"]
                pool.remove(old)
            pool.append(it)
        return sends, nsend, nrecv

    def run(self):
        ops = self.order()
        rest, nsend, nrecv = self.semaphores(ops)
        assert nsend <= NSEND and nrecv <= NRECV, (nsend, nrecv)
        for what, it in ops:
            if what == "step":
                it["fn"]()
            elif what == "recv":
                it["wait"].wait_recv()
                if it["land"] is not None:
                    it["land"]()
            else:
                if it["before"] is not None:
                    it["before"]()
                if it["after"] is not None:
                    it["after"]["copy"].wait_send()
                it["copy"], it["wait"] = (
                    pltpu.make_async_remote_copy(
                        s, d, self.ssem.at[it["ssem"]], self.rsem.at[it["rsem"]],
                        device_id=self.devs[it["link"]], device_id_type=MESH,
                    )
                    for s, d in ((it["src"], it["dst"]), (it["arrive"], it["arrive"]))
                )
                it["copy"].start()
        for it in rest:
            it["copy"].wait_send()


def kernel(
    ui_h, di_h, x_h, c_h, up_h, dn_h,
    ig_out, gu_out, gd_out,
    xo, xp0, xp1, w, g, act, gpre, terms, ig,
    rau, rad, rbu, rbd, rx, rax, rc, cs, ryu, ryd, rp, wuh, wul, slot, ui, di,
    lsem, ssem, rsem,
):
    t, h = lax.axis_index("tok"), lax.axis_index("hid")
    z, x = t // NX, lax.rem(t, NX)
    y, c = h // 2, lax.rem(h, 2)
    hf = x // 2
    j = jnp.where((x == 1) | (x == 2), 1, 0)
    zz = lambda d: lax.rem(z + d + NZ, NZ)
    yy = lambda d: lax.rem(y + d + NY, NY)
    tok = lambda tz, tx: tz * NX + tx
    devs = {
        "cross": (tok(z, 3 - x), h),
        "in": (tok(z, x + 1 - 2 * lax.rem(x, 2)), h),
        "zu": (tok(zz(1), x), h),
        "zd": (tok(zz(-1), x), h),
        "yu": (t, yy(1) * 2 + c),
        "yd": (t, yy(-1) * 2 + c),
        "core": (t, y * 2 + 1 - c),
    }
    barrier = pltpu.get_barrier_semaphore()
    for dev in devs.values():
        pl.semaphore_signal(barrier, inc=1, device_id=dev, device_id_type=MESH)

    def local(n, src, dst):
        cp = pltpu.make_async_copy(src, dst, lsem.at[n])
        cp.start()
        return cp

    li = [local(4, ui_h, ui), local(5, di_h, di)]
    lw = [
        local(0, up_h.at[pl.ds(NF * hf, NF)], w.at[z, j, hf, 0]),
        local(1, dn_h.at[pl.ds(NF * hf, NF)], w.at[z, j, hf, 1]),
    ]
    lx = [local(2, x_h, xo.at[0]), local(3, c_h, xo.at[1])]
    for cp in lw:
        cp.wait()
    pl.semaphore_wait(barrier, len(devs))

    p = Plan(ssem, rsem, devs)
    HZ = NZ // 2
    js, ms = (j, 1 - j), (hf, 1 - hf)
    oh = NF * (1 - hf)
    KF = 2 * 8192

    def weight_gather(q, rank):
        (a0, an), (b0, bn) = CHUNKS[q]
        A, B = pl.ds(a0, an), pl.ds(b0, bn)
        wA = lambda d, a, m: w.at[zz(d), js[a], ms[m], :, A]
        wB = lambda d, a, m: w.at[zz(d), js[a], ms[m], :, B]
        need = []

        def ring(tag, ref, size, m, deps0, rank):
            have = {0: deps0}
            for s in range(HZ):
                for link, sg in (("zu", -1), ("zd", 1)):
                    if s == HZ - 1 and (m == 0) != (link == "zu"):
                        continue
                    name = f"g{q}{tag}{m}{link}{s}"
                    p.send(name, link, ref(sg * s), ref(sg * s), ref(sg * (s + 1)), size, have[sg * s], rank=rank)
                    have[HZ if s == HZ - 1 else sg * (s + 1)] = [name]
                    need.append(name)
            return have

        for m in range(2):
            w0a, w0b = ([], []) if m == 0 else ([f"w{q}a0", f"w{q}a1"], [f"w{q}b0", f"w{q}b1"])
            p.send(f"ax{q}{m}", "in", wA(0, 0, m), wA(0, 0, m), wA(0, 1, m), an * KF, w0a, rank=rank - 0.5)
            need.append(f"ax{q}{m}")
            hb = ring("b", lambda d, m=m: wB(d, 0, m), bn * KF, m, w0b, rank + 0.15 - 0.1 * m)
            for d in (0, -1, 1, -2, 2, -3, 3, HZ):
                p.send(f"bx{q}{m}{d}", "in", wB(d, 0, m), wB(d, 0, m), wB(d, 1, m), bn * KF, hb[d], rank=rank)
                need.append(f"bx{q}{m}{d}")
            ring("a", lambda d, m=m: wA(d, 0, m), an * KF, m, w0a, rank + 0.3 - 0.1 * m)
            ring("o", lambda d, m=m: wA(d, 1, m), an * KF, m, [f"ax{q}{m}"], rank + 0.1 - 0.1 * m)
            if m == 0:
                for tag, F, lo_f, n_f in (("b", B, b0, bn), ("a", A, a0, an)):
                    for e, ref in enumerate((up_h, dn_h)):
                        p.send(
                            f"w{q}{tag}{e}", "cross", ref.at[pl.ds(oh + lo_f, n_f)],
                            w.at[z, j, hf, e, F], w.at[z, j, 1 - hf, e, F], n_f * 8192, rank=rank - 0.1 * (tag == "a"),
                        )
        return need

    need_w = [weight_gather(0, 0), weight_gather(1, 2)]

    RH = 4
    need_t = [], []
    KT = RH * 8 * 512 * 4

    def share(m, r, ty, tc, sub=None):
        rows = pl.ds(r * RH, RH) if sub is None else pl.ds(r * RH + sub * (RH // 2), RH // 2)
        return (xp0, xp1)[m].at[rows, pl.ds((tc * NY + ty) * 4, 4)]

    for m in range(2):
        for r in range(16 // RH):
            k = f"{m}{r}"
            sh = lambda d, q=c, sub=None, m=m, r=r: share(m, r, yy(d), q, sub)
            src = (x_h, c_h)[m].at[pl.ds(r * RH, RH), pl.ds((c * NY + y) * 4, 4)]
            p.send(f"t{k}", "cross", src, sh(0), sh(0), KT, rank=1 if r + 4 * m < 4 else 3)
            p.send(f"tyu{k}", "yu", sh(0), sh(0), sh(-1), KT, [f"t{k}"])
            p.send(f"tyd{k}", "yd", sh(0), sh(0), sh(1), KT, [f"t{k}"])
            p.send(f"tzu{k}", "yu", sh(-1, c, 0), sh(-1, c, 0), sh(-2, c, 0), KT // 2, [f"tyu{k}"])
            p.send(f"tzd{k}", "yd", sh(1, c, 1), sh(1, c, 1), sh(2, c, 1), KT // 2, [f"tyd{k}"])
            for d, dep in ((0, [f"t{k}"]), (-1, [f"tyu{k}"]), (1, [f"tyd{k}"]), (2, [f"tzu{k}", f"tzd{k}"])):
                p.send(f"tc{k}{d}", "core", sh(d), sh(d), sh(d, 1 - c), KT, dep)
                need_t[m].append(f"tc{k}{d}")

    def make_slots():
        for cp in li:
            cp.wait()
        for i in range(NF):
            picks = [ui[k, NF * hf + i] for k in range(4)]

            def one(b, carry, i=i, picks=picks):
                v = jnp.int32(4 * NF)
                for k in range(4):
                    v = jnp.where(picks[k] == b, 4 * i + k, v)
                slot[i, b] = v
                return carry

            lax.fori_loop(0, 32, one, 0)
        terms[4 * NF] = jnp.zeros((256, 128), F32)

    p.step("slots", 0.5, make_slots)
    lo = lax.broadcasted_iota(jnp.int32, (NZ, 8, 128), 1) < 4

    def weights(m, i):
        out = []
        for kp in range(2):
            x0, x3, x1, x2 = (w[:, jj, mm, m, i, kp] for jj in range(2) for mm in range(2))
            a0, b0 = merge4(lo, x0, x1)
            a1, b1 = merge4(lo, x2, x3)
            out += [jnp.stack([a0, a1], 1).reshape(128, 128), jnp.stack([b0, b1], 1).reshape(128, 128)]
        return out

    def tokens(m, idx, i):
        cols = []
        for k in range(4):
            b = idx[k, NF * hf + i]
            cols.append(jnp.concatenate([xo[m, :, b].reshape(128, 128), (xp0, xp1)[m][:, b].reshape(128, 128)], 0))
        return split(jnp.concatenate(cols, 1))

    def before(i):
        wh, wl = split(jnp.concatenate(weights(0, i), 0))
        wuh[i], wul[i] = wh, wl
        xh, xl = tokens(0, ui, i)
        act[i] = fold(dot(xh, jnp.concatenate([wh, wl], 1), ((1,), (0,)))) + dot(xl, wh, ((1,), (0,)))

    def after(i):
        wh, wl = split(jnp.concatenate(weights(1, i), 1))
        ch, cl = tokens(1, di, i)
        ga = fold(dot(ch, jnp.concatenate([wh, wl], 0), ((1,), (1,)))) + dot(cl, wh, ((1,), (1,)))
        pre = act[i]
        sg = 1.0 / (1.0 + jnp.exp(-pre))
        act[i] = pre * sg
        gp = ga * sg * (1.0 + pre * (1.0 - sg))
        gpre[i] = gp
        gh, gl = split(gp)
        uh, ul = wuh[i], wul[i]
        back = dot(jnp.concatenate([gh, gl], 1), jnp.concatenate([uh, uh], 1), ((1,), (1,))) + dot(gh, ul, ((1,), (1,)))
        for k in range(4):
            terms[i * 4 + k] = back[:, k * 128 : (k + 1) * 128]

    def gather_terms(b, carry):
        total = terms[slot[0, b]]
        for i in range(1, NF):
            total = total + terms[slot[i, b]]
        ig[b // 8, lax.rem(b // 4, 2), lax.rem(b, 4)] = total
        return carry

    def grads(i, carry):
        gh, gl = split(gpre[i])
        ah, al = split(act[i])
        xh, xl = tokens(0, ui, i)
        ch, cl = tokens(1, di, i)
        d00 = ((0,), (0,))
        gu = fold(dot(xh, jnp.concatenate([gh, gl], 1), d00)) + dot(xl, gh, d00)
        gd = dot(ah, ch, d00) + dot(ah, cl, d00) + dot(al, ch, d00)
        for m, full in enumerate((gu, gd)):
            for kp in range(2):
                if m == 0:
                    k0, k1 = (full[(2 * kp + e) * 128 : (2 * kp + e + 1) * 128] for e in range(2))
                else:
                    k0, k1 = (full[:, (2 * kp + e) * 128 : (2 * kp + e + 1) * 128] for e in range(2))
                k0, k1 = k0.reshape(NZ, 2, 8, 128), k1.reshape(NZ, 2, 8, 128)
                x0, x1 = merge4(lo, k0[:, 0], k1[:, 0])
                x2, x3 = merge4(lo, k0[:, 1], k1[:, 1])
                g[:, 0, 0, m, i, kp] = x0
                g[:, 1, 0, m, i, kp] = x1
                g[:, 1, 1, m, i, kp] = x2
                g[:, 0, 1, m, i, kp] = x3
        return carry

    loop = lambda a, b, fn: lambda: lax.fori_loop(a, b, fn, 0) and None

    def wait_own():
        for cp in lx:
            cp.wait()

    p.step("own", 0.1, wait_own)
    chunk_fs = [[f for f0, n in ch for f in range(f0, f0 + n)] for ch in CHUNKS]
    for q, fs in enumerate(chunk_fs):
        for i in fs:
            p.step(f"pre{i}", 0.45, functools.partial(before, i), need_w[q] + need_t[0] + ["own", "slots"], rank=10 + 2 * q)
            p.step(f"fwd{i}", 0.75, functools.partial(after, i), [f"pre{i}"] + need_t[1], rank=10 + 2 * q)
        p.step(f"grad{q}", 0.5 * len(fs), [loop(f0, f0 + n, grads) for f0, n in ((fs[0], len(fs)),)][0],
               [f"fwd{i}" for i in fs] + (["terms"] if q else []), rank=11 + 3 * q)
    p.step("terms", 0.5, loop(0, 32, gather_terms), [f"fwd{i}" for i in range(NF)], rank=13)

    KI = 256 * 128 * 4

    def add_ig(d, b, buf):
        def fn():
            ig[yy(d), c, b] += buf[...]

        return fn

    for n, d in enumerate((2, 1, -1, 0)):
        for b in range(4):
            buf = cs.at[n, b]
            p.send(f"c{d}{b}", "core", ig.at[yy(d), 1 - c, b], buf, buf, KI, ["terms"], add_ig(d, b, buf), rank=20 + b % 2)
    for b in range(4):
        for link, sg, buf in (("yu", 1, ryu), ("yd", -1, ryd)):
            dep, before = [f"c{sg}{b}"], None
            if (b < 2) == (link == "yu"):
                p.send(f"y2{b}", link, ig.at[yy(2), c, b], buf.at[0, b], buf.at[0, b], KI, [f"c2{b}"], rank=20 + b % 2)
                dep.append(f"y2{b}")
                before = add_ig(sg, b, buf.at[0, b])
            p.send(f"y1{link}{b}", link, ig.at[yy(sg), c, b], buf.at[1, b], buf.at[1, b], KI, dep, None, before, rank=20 + b % 2)

    def ig_sum(b):
        def fn():
            ig[y, c, b] += ryu[1, b] + ryd[1, b]

        return fn

    def ig_final(b):
        def fn():
            ig_out[:, b * 128 : (b + 1) * 128] = ig[y, c, b, 0:128] + rp[b]

        return fn

    for b in range(4):
        p.send(
            f"p{b}", "cross", ig.at[y, c, b, pl.ds(128, 128)], rp.at[b], rp.at[b], KI // 2,
            [f"y1yu{b}", f"y1yd{b}", f"c0{b}"], ig_final(b), ig_sum(b), rank=20,
        )

    zorder = (HZ, 3, -3, 2, -2, 1, -1, 0)

    def add_to(ref, buf):
        def fn():
            ref[...] += buf[...]

        return fn

    def add2(ref, b1, b2):
        def fn():
            ref[...] += b1[...] + b2[...]

        return fn

    def weight_reduce(q, rank):
        (a0, an), (b0, bn) = CHUNKS[q]
        A, B = pl.ds(a0, an), pl.ds(b0, bn)
        ready = [f"grad{q}"]
        gA = lambda d, a, m: g.at[zz(d), js[a], ms[m], :, A]
        gB = lambda d, a, m: g.at[zz(d), js[a], ms[m], :, B]
        for n, d in enumerate(zorder):
            for m in range(2):
                buf = rx.at[n, ms[m], :, B]
                p.send(f"rx{q}{m}{d}", "in", gB(d, 1, m), buf, buf, bn * KF, ready, add_to(gB(d, 0, m), buf), rank=rank)

        def ring(tag, ref, bufs, size, m, deps, rank):
            for s in range(HZ):
                for link, sg in (("zu", 1), ("zd", -1)):
                    if s == 0 and (m == 0) != (link == "zu"):
                        continue
                    d = sg * (HZ - s)
                    dep, before = list(deps(HZ if s == 0 else d)), None
                    if s > 1 or (s == 1 and (m == 0) == (link == "zu")):
                        dep.append(f"r{q}{tag}{m}{link}{s - 1}")
                        before = add_to(ref(d), bufs[link](s - 1))
                    p.send(f"r{q}{tag}{m}{link}{s}", link, ref(d), bufs[link](s), bufs[link](s), size, dep, None, before, rank=rank)
            return [f"r{q}{tag}{m}{link}{HZ - 1}" for link in ("zu", "zd")]

        for m in range(2):
            bufs = {
                "zu": lambda s, m=m: rbu.at[s, ms[m], :, B],
                "zd": lambda s, m=m: rbd.at[s, ms[m], :, B],
            }
            fin = ring("B", lambda d, m=m: gB(d, 0, m), bufs, bn * KF, m, lambda d, m=m: [f"rx{q}{m}{d}"], rank)
            p.step(f"finB{q}{m}", 0.05, add2(gB(0, 0, m), bufs["zu"](HZ - 1), bufs["zd"](HZ - 1)), fin + [f"rx{q}{m}0"])
        for m in range(2):
            for a in (1, 0):
                bufs = {
                    "zu": lambda s, m=m, a=a: rau.at[s, js[a], ms[m], :, A],
                    "zd": lambda s, m=m, a=a: rad.at[s, js[a], ms[m], :, A],
                }
                tag = "AO"[a]
                fin = ring(tag, lambda d, m=m, a=a: gA(d, a, m), bufs, an * KF, m, lambda d: ready, rank + 5)
                p.step(f"fin{tag}{q}{m}", 0.05, add2(gA(0, a, m), bufs["zu"](HZ - 1), bufs["zd"](HZ - 1)), fin)
            buf = rax.at[ms[m], :, A]
            p.send(f"rax{q}{m}", "in", gA(0, 1, m), buf, buf, an * KF, [f"finO{q}{m}"], rank=rank - 1)
            p.step(f"sumA{q}{m}", 0.05, add_to(gA(0, 0, m), buf), [f"rax{q}{m}", f"finA{q}{m}"])
        p.send(f"cB{q}", "cross", g.at[z, j, 1 - hf, :, B], rc.at[:, B], rc.at[:, B], bn * KF, [f"finB{q}1"], rank=rank)
        p.send(f"cA{q}", "cross", g.at[z, j, 1 - hf, :, A], rc.at[:, A], rc.at[:, A], an * KF, [f"sumA{q}1"], rank=rank)
        return [f"finB{q}0", f"sumA{q}0"], [f"cB{q}", f"cA{q}"]

    outs = [weight_reduce(0, 30), weight_reduce(1, 32)]

    def own_out():
        for m, out in enumerate((gu_out, gd_out)):
            out[pl.ds(NF * hf, NF)] = g[z, j, hf, m]

    def other_out():
        for m, out in enumerate((gu_out, gd_out)):
            out[pl.ds(oh, NF)] = rc[m]

    p.step("own_out", 0.1, own_out, outs[0][0] + outs[1][0])
    p.step("other_out", 0.1, other_out, outs[0][1] + outs[1][1])
    p.run()


def finish(ig, gu, gd, mu, md, ig_out, mu_out, md_out):
    ig_out[...] = ig[...]
    mu_out[...] = 0.9 * mu[...] + (1.0 / 64.0) * gu[...]
    md_out[...] = 0.9 * md[...] + (1.0 / 64.0) * gd[...]


def shards(inputs, cotangent, up_blocks, down_blocks, up_index, down_index, mom_up, mom_down):
    f, kb, r, b = up_blocks.shape
    tiles = lambda a: a.reshape(f, kb // 2, 2 * r, b)
    rows8 = lambda a: a.reshape(16, 8, 32, b).transpose(0, 2, 1, 3)
    vm = lambda *s: pltpu.VMEM(s, F32)
    hbm = pl.BlockSpec(memory_space=pl.ANY)
    vmem = pl.BlockSpec(memory_space=pltpu.VMEM)
    tile = (2, 8, 128)
    out_shape = (
        jax.ShapeDtypeStruct((128, 512), F32),
        jax.ShapeDtypeStruct((f, *tile), F32),
        jax.ShapeDtypeStruct((f, *tile), F32),
    )
    ig, gu, gd = pl.pallas_call(
        kernel,
        out_shape=tuple(vm(*o.shape) for o in out_shape),
        in_specs=[hbm] * 6,
        out_specs=(vmem, vmem, vmem),
        scratch_shapes=[
            vm(2, 16, 32, 8, 128),
            vm(16, 32, 8, 128),
            vm(16, 32, 8, 128),
            vm(NZ, 2, 2, 2, NF, *tile),
            vm(NZ, 2, 2, 2, NF, *tile),
            vm(NF, 256, 128),
            vm(NF, 256, 128),
            vm(4 * NF + 1, 256, 128),
            vm(NY, 2, 4, 256, 128),
            vm(NZ // 2, 2, 2, 2, NF, *tile),
            vm(NZ // 2, 2, 2, 2, NF, *tile),
            vm(NZ // 2, 2, 2, NF, *tile),
            vm(NZ // 2, 2, 2, NF, *tile),
            vm(NZ, 2, 2, NF, *tile),
            vm(2, 2, NF, *tile),
            vm(2, NF, *tile),
            vm(NY, 4, 256, 128),
            vm(2, 4, 256, 128),
            vm(2, 4, 256, 128),
            vm(4, 128, 128),
            pltpu.VMEM((NF, 512, 128), BF),
            pltpu.VMEM((NF, 512, 128), BF),
            pltpu.SMEM((NF, 32), jnp.int32),
            pltpu.SMEM((kb, f), jnp.int32),
            pltpu.SMEM((kb, f), jnp.int32),
            pltpu.SemaphoreType.DMA((6,)),
            pltpu.SemaphoreType.DMA((NSEND,)),
            pltpu.SemaphoreType.DMA((NRECV,)),
        ],
        compiler_params=pltpu.CompilerParams(
            collective_id=0, has_side_effects=True, vmem_limit_bytes=60 * 1024 * 1024
        ),
    )(up_index.T, down_index.T, rows8(inputs), rows8(cotangent), tiles(up_blocks), tiles(down_blocks))
    ig, mu, md = pl.pallas_call(finish, out_shape=out_shape, in_specs=[vmem] * 5, out_specs=(vmem,) * 3)(
        *(pltpu.with_memory_space_constraint(a, pltpu.VMEM) for a in (ig, gu, gd)), tiles(mom_up), tiles(mom_down)
    )
    return ig, mu.reshape(mom_up.shape), md.reshape(mom_down.shape)


def solution(mesh):
    return jax.shard_map(
        shards,
        mesh=mesh,
        in_specs=(
            P("tok", None),
            P("tok", None),
            P("hid", None, "tok", None),
            P("hid", None, "tok", None),
            P("hid", None),
            P("hid", None),
            P("hid", None, "tok", None),
            P("hid", None, "tok", None),
        ),
        out_specs=(P("tok", "hid"), P("hid", None, "tok", None), P("hid", None, "tok", None)),
        check_vma=False,
    )
```

```python
import functools
import heapq

import jax
import jax.numpy as jnp
from jax import lax
from jax.experimental import pallas as pl
from jax.experimental.pallas import tpu as pltpu
from jax.sharding import PartitionSpec as P

MESH = pl.DeviceIdType.MESH
NX, NY, NZ = 4, 4, 8
NF = 7
CHUNKS = (((0, 2), (2, 2)), ((4, 1), (5, 2)))
NSEND, NRECV = 38, 94
DEPTH = 1.5
BF, F32 = jnp.bfloat16, jnp.float32


def split(a):
    hi = a.astype(BF)
    return hi, (a - hi.astype(F32)).astype(BF)


def dot(a, b, dims):
    return lax.dot_general(a, b, (dims, ((), ())), preferred_element_type=F32)


def fold(a):
    return a[:, :128] + a[:, 128:]


def merge4(lo, a, b):
    ra, rb = pltpu.roll(a, 4, 1), pltpu.roll(b, 4, 1)
    return jnp.where(lo, a, rb), jnp.where(lo, ra, b)


class Plan:
    RATE = {"core": 500.0}
    LAT = {"core": 1.0, "cross": 1.9, "in": 1.9, "yu": 1.9, "yd": 1.9, "zu": 2.2, "zd": 2.2}

    def __init__(self, ssem, rsem, devs):
        self.ssem, self.rsem, self.devs = ssem, rsem, devs
        self.items = []

    def send(self, name, link, src, dst, arrive, size, deps=(), land=None, before=None, rank=0):
        self.items.append(
            dict(name=name, link=link, src=src, dst=dst, arrive=arrive, size=size, deps=set(deps), land=land, before=before, rank=rank)
        )

    def step(self, name, cost, fn, deps=(), rank=0):
        self.items.append(dict(name=name, link=None, cost=cost, fn=fn, deps=set(deps), rank=rank))

    def order(self):
        now, free, done, flying, tick, ops = 0.0, {}, set(), [], 0, []
        todo = sorted(self.items, key=lambda i: i["rank"])
        while todo or flying:
            for it in [i for i in todo if i["link"] and i["deps"] <= done]:
                if free.get(it["link"], 0.0) - now > DEPTH:
                    continue
                todo.remove(it)
                end = max(now, free.get(it["link"], 0.0)) + it["size"] / 1e3 / self.RATE.get(it["link"], 46.0)
                free[it["link"]] = it["end"] = end
                it["start"] = now
                ops.append(("send", it))
                heapq.heappush(flying, (end + self.LAT[it["link"]], tick, it))
                tick += 1
            ready = next((i for i in todo if not i["link"] and i["deps"] <= done), None)
            if ready is not None and not (flying and flying[0][0] <= now):
                todo.remove(ready)
                ops.append(("step", ready))
                now += ready["cost"]
                done.add(ready["name"])
                continue
            when, _, it = heapq.heappop(flying)
            now = max(now, when)
            ops.append(("recv", it))
            done.add(it["name"])
        return ops

    def semaphores(self, ops):
        back = {"zu": "zd", "zd": "zu", "yu": "yd", "yd": "yu"}
        sent_at = {id(it): n for n, (what, it) in enumerate(ops) if what == "send"}
        got_at = {id(it): n for n, (what, it) in enumerate(ops) if what == "recv"}
        nsend, nrecv, sends, recvs = 0, 0, [], {}
        for n, (what, it) in enumerate(ops):
            if what != "send":
                continue
            it["after"] = None
            old = next((o for o in sends if o["end"] + 2.0 < it["start"]), None)
            if old is None:
                it["ssem"] = nsend
                nsend += 1
            else:
                it["ssem"], it["after"] = old["ssem"], old
                sends.remove(old)
            sends.append(it)
            link = it["link"]
            echo = [sent_at[id(o)] for w2, o in ops[:n] if w2 == "recv" and o["link"] == back.get(link, link)]
            last = max(echo, default=-1)
            pool = recvs.setdefault(link, [])
            old = next((o for o in pool if got_at[id(o)] < last), None)
            if old is None:
                it["rsem"] = nrecv
                nrecv += 1
            else:
                it["rsem"] = old["rsem"]
                pool.remove(old)
            pool.append(it)
        return sends, nsend, nrecv

    def run(self):
        ops = self.order()
        rest, nsend, nrecv = self.semaphores(ops)
        assert nsend <= NSEND and nrecv <= NRECV, (nsend, nrecv)
        for what, it in ops:
            if what == "step":
                it["fn"]()
            elif what == "recv":
                it["wait"].wait_recv()
                if it["land"] is not None:
                    it["land"]()
            else:
                if it["before"] is not None:
                    it["before"]()
                if it["after"] is not None:
                    it["after"]["copy"].wait_send()
                it["copy"], it["wait"] = (
                    pltpu.make_async_remote_copy(
                        s, d, self.ssem.at[it["ssem"]], self.rsem.at[it["rsem"]],
                        device_id=self.devs[it["link"]], device_id_type=MESH,
                    )
                    for s, d in ((it["src"], it["dst"]), (it["arrive"], it["arrive"]))
                )
                it["copy"].start()
        for it in rest:
            it["copy"].wait_send()


def kernel(
    ui_h, di_h, x_h, c_h, up_h, dn_h, mu_h, md_h,
    ig_out, gu_out, gd_out,
    xo, xp0, xp1, w, g, act, gpre, terms, ig,
    rau, rad, rbu, rbd, rx, rax, rc, cs, ryu, ryd, rp, wuh, wul, slot, ui, di, mom,
    lsem, ssem, rsem,
):
    t, h = lax.axis_index("tok"), lax.axis_index("hid")
    z, x = t // NX, lax.rem(t, NX)
    y, c = h // 2, lax.rem(h, 2)
    hf = x // 2
    j = jnp.where((x == 1) | (x == 2), 1, 0)
    zz = lambda d: lax.rem(z + d + NZ, NZ)
    yy = lambda d: lax.rem(y + d + NY, NY)
    tok = lambda tz, tx: tz * NX + tx
    devs = {
        "cross": (tok(z, 3 - x), h),
        "in": (tok(z, x + 1 - 2 * lax.rem(x, 2)), h),
        "zu": (tok(zz(1), x), h),
        "zd": (tok(zz(-1), x), h),
        "yu": (t, yy(1) * 2 + c),
        "yd": (t, yy(-1) * 2 + c),
        "core": (t, y * 2 + 1 - c),
    }
    barrier = pltpu.get_barrier_semaphore()
    for dev in devs.values():
        pl.semaphore_signal(barrier, inc=1, device_id=dev, device_id_type=MESH)

    def local(n, src, dst):
        cp = pltpu.make_async_copy(src, dst, lsem.at[n])
        cp.start()
        return cp

    lm = [local(6, mu_h, mom.at[0]), local(7, md_h, mom.at[1])]
    li = [local(4, ui_h, ui), local(5, di_h, di)]
    lw = [
        local(0, up_h.at[pl.ds(NF * hf, NF)], w.at[z, j, hf, 0]),
        local(1, dn_h.at[pl.ds(NF * hf, NF)], w.at[z, j, hf, 1]),
    ]
    lx = [local(2, x_h, xo.at[0]), local(3, c_h, xo.at[1])]
    for cp in lw:
        cp.wait()
    pl.semaphore_wait(barrier, len(devs))

    p = Plan(ssem, rsem, devs)
    HZ = NZ // 2
    js, ms = (j, 1 - j), (hf, 1 - hf)
    oh = NF * (1 - hf)
    KF = 2 * 8192

    def weight_gather(q, rank):
        (a0, an), (b0, bn) = CHUNKS[q]
        A, B = pl.ds(a0, an), pl.ds(b0, bn)
        wA = lambda d, a, m: w.at[zz(d), js[a], ms[m], :, A]
        wB = lambda d, a, m: w.at[zz(d), js[a], ms[m], :, B]
        need = []

        def ring(tag, ref, size, m, deps0, rank):
            have = {0: deps0}
            for s in range(HZ):
                for link, sg in (("zu", -1), ("zd", 1)):
                    if s == HZ - 1 and (m == 0) != (link == "zu"):
                        continue
                    name = f"g{q}{tag}{m}{link}{s}"
                    p.send(name, link, ref(sg * s), ref(sg * s), ref(sg * (s + 1)), size, have[sg * s], rank=rank)
                    have[HZ if s == HZ - 1 else sg * (s + 1)] = [name]
                    need.append(name)
            return have

        for m in range(2):
            w0a, w0b = ([], []) if m == 0 else ([f"w{q}a0", f"w{q}a1"], [f"w{q}b0", f"w{q}b1"])
            p.send(f"ax{q}{m}", "in", wA(0, 0, m), wA(0, 0, m), wA(0, 1, m), an * KF, w0a, rank=rank - 0.5)
            need.append(f"ax{q}{m}")
            hb = ring("b", lambda d, m=m: wB(d, 0, m), bn * KF, m, w0b, rank + 0.15 - 0.1 * m)
            for d in (0, -1, 1, -2, 2, -3, 3, HZ):
                p.send(f"bx{q}{m}{d}", "in", wB(d, 0, m), wB(d, 0, m), wB(d, 1, m), bn * KF, hb[d], rank=rank)
                need.append(f"bx{q}{m}{d}")
            ring("a", lambda d, m=m: wA(d, 0, m), an * KF, m, w0a, rank + 0.3 - 0.1 * m)
            ring("o", lambda d, m=m: wA(d, 1, m), an * KF, m, [f"ax{q}{m}"], rank + 0.1 - 0.1 * m)
            if m == 0:
                for tag, F, lo_f, n_f in (("b", B, b0, bn), ("a", A, a0, an)):
                    for e, ref in enumerate((up_h, dn_h)):
                        p.send(
                            f"w{q}{tag}{e}", "cross", ref.at[pl.ds(oh + lo_f, n_f)],
                            w.at[z, j, hf, e, F], w.at[z, j, 1 - hf, e, F], n_f * 8192, rank=rank - 0.1 * (tag == "a"),
                        )
        return need

    need_w = [weight_gather(0, 0), weight_gather(1, 2)]

    RH = 4
    need_t = [], []
    KT = RH * 8 * 512 * 4

    def share(m, r, ty, tc, sub=None):
        rows = pl.ds(r * RH, RH) if sub is None else pl.ds(r * RH + sub * (RH // 2), RH // 2)
        return (xp0, xp1)[m].at[rows, pl.ds((tc * NY + ty) * 4, 4)]

    for m in range(2):
        for r in range(16 // RH):
            k = f"{m}{r}"
            sh = lambda d, q=c, sub=None, m=m, r=r: share(m, r, yy(d), q, sub)
            src = (x_h, c_h)[m].at[pl.ds(r * RH, RH), pl.ds((c * NY + y) * 4, 4)]
            p.send(f"t{k}", "cross", src, sh(0), sh(0), KT, rank=1 if r + 4 * m < 4 else 3)
            p.send(f"tyu{k}", "yu", sh(0), sh(0), sh(-1), KT, [f"t{k}"])
            p.send(f"tyd{k}", "yd", sh(0), sh(0), sh(1), KT, [f"t{k}"])
            p.send(f"tzu{k}", "yu", sh(-1, c, 0), sh(-1, c, 0), sh(-2, c, 0), KT // 2, [f"tyu{k}"])
            p.send(f"tzd{k}", "yd", sh(1, c, 1), sh(1, c, 1), sh(2, c, 1), KT // 2, [f"tyd{k}"])
            for d, dep in ((0, [f"t{k}"]), (-1, [f"tyu{k}"]), (1, [f"tyd{k}"]), (2, [f"tzu{k}", f"tzd{k}"])):
                p.send(f"tc{k}{d}", "core", sh(d), sh(d), sh(d, 1 - c), KT, dep)
                need_t[m].append(f"tc{k}{d}")

    def make_slots():
        for cp in li:
            cp.wait()
        for i in range(NF):
            picks = [ui[k, NF * hf + i] for k in range(4)]

            def one(b, carry, i=i, picks=picks):
                v = jnp.int32(4 * NF)
                for k in range(4):
                    v = jnp.where(picks[k] == b, 4 * i + k, v)
                slot[i, b] = v
                return carry

            lax.fori_loop(0, 32, one, 0)
        terms[4 * NF] = jnp.zeros((256, 128), F32)

    p.step("slots", 0.5, make_slots)
    lo = lax.broadcasted_iota(jnp.int32, (NZ, 8, 128), 1) < 4

    def weights(m, i):
        out = []
        for kp in range(2):
            x0, x3, x1, x2 = (w[:, jj, mm, m, i, kp] for jj in range(2) for mm in range(2))
            a0, b0 = merge4(lo, x0, x1)
            a1, b1 = merge4(lo, x2, x3)
            out += [jnp.stack([a0, a1], 1).reshape(128, 128), jnp.stack([b0, b1], 1).reshape(128, 128)]
        return out

    def tokens(m, idx, i):
        cols = []
        for k in range(4):
            b = idx[k, NF * hf + i]
            cols.append(jnp.concatenate([xo[m, :, b].reshape(128, 128), (xp0, xp1)[m][:, b].reshape(128, 128)], 0))
        return split(jnp.concatenate(cols, 1))

    def before(i):
        wh, wl = split(jnp.concatenate(weights(0, i), 0))
        wuh[i], wul[i] = wh, wl
        xh, xl = tokens(0, ui, i)
        act[i] = fold(dot(xh, jnp.concatenate([wh, wl], 1), ((1,), (0,)))) + dot(xl, wh, ((1,), (0,)))

    def after(i):
        wh, wl = split(jnp.concatenate(weights(1, i), 1))
        ch, cl = tokens(1, di, i)
        ga = fold(dot(ch, jnp.concatenate([wh, wl], 0), ((1,), (1,)))) + dot(cl, wh, ((1,), (1,)))
        pre = act[i]
        sg = 1.0 / (1.0 + jnp.exp(-pre))
        act[i] = pre * sg
        gp = ga * sg * (1.0 + pre * (1.0 - sg))
        gpre[i] = gp
        gh, gl = split(gp)
        uh, ul = wuh[i], wul[i]
        back = dot(jnp.concatenate([gh, gl], 1), jnp.concatenate([uh, uh], 1), ((1,), (1,))) + dot(gh, ul, ((1,), (1,)))
        for k in range(4):
            terms[i * 4 + k] = back[:, k * 128 : (k + 1) * 128]

    def gather_terms(b, carry):
        total = terms[slot[0, b]]
        for i in range(1, NF):
            total = total + terms[slot[i, b]]
        ig[b // 8, lax.rem(b // 4, 2), lax.rem(b, 4)] = total
        return carry

    def grads(i, carry):
        gh, gl = split(gpre[i])
        ah, al = split(act[i])
        xh, xl = tokens(0, ui, i)
        ch, cl = tokens(1, di, i)
        d00 = ((0,), (0,))
        gu = fold(dot(xh, jnp.concatenate([gh, gl], 1), d00)) + dot(xl, gh, d00)
        gd = dot(ah, ch, d00) + dot(ah, cl, d00) + dot(al, ch, d00)
        for m, full in enumerate((gu, gd)):
            for kp in range(2):
                if m == 0:
                    k0, k1 = (full[(2 * kp + e) * 128 : (2 * kp + e + 1) * 128] for e in range(2))
                else:
                    k0, k1 = (full[:, (2 * kp + e) * 128 : (2 * kp + e + 1) * 128] for e in range(2))
                k0, k1 = k0.reshape(NZ, 2, 8, 128), k1.reshape(NZ, 2, 8, 128)
                x0, x1 = merge4(lo, k0[:, 0], k1[:, 0])
                x2, x3 = merge4(lo, k0[:, 1], k1[:, 1])
                g[:, 0, 0, m, i, kp] = x0
                g[:, 1, 0, m, i, kp] = x1
                g[:, 1, 1, m, i, kp] = x2
                g[:, 0, 1, m, i, kp] = x3
        return carry

    loop = lambda a, b, fn: lambda: lax.fori_loop(a, b, fn, 0) and None

    def wait_own():
        for cp in lx:
            cp.wait()

    p.step("own", 0.1, wait_own)
    chunk_fs = [[f for f0, n in ch for f in range(f0, f0 + n)] for ch in CHUNKS]
    for q, fs in enumerate(chunk_fs):
        for i in fs:
            p.step(f"pre{i}", 0.45, functools.partial(before, i), need_w[q] + need_t[0] + ["own", "slots"], rank=10 + 2 * q)
            p.step(f"fwd{i}", 0.75, functools.partial(after, i), [f"pre{i}"] + need_t[1], rank=10 + 2 * q)
        p.step(f"grad{q}", 0.5 * len(fs), [loop(f0, f0 + n, grads) for f0, n in ((fs[0], len(fs)),)][0],
               [f"fwd{i}" for i in fs] + (["terms"] if q else []), rank=11 + 3 * q)
    p.step("terms", 0.5, loop(0, 32, gather_terms), [f"fwd{i}" for i in range(NF)], rank=13)

    KI = 256 * 128 * 4

    def add_ig(d, b, buf):
        def fn():
            ig[yy(d), c, b] += buf[...]

        return fn

    for n, d in enumerate((2, 1, -1, 0)):
        for b in range(4):
            buf = cs.at[n, b]
            p.send(f"c{d}{b}", "core", ig.at[yy(d), 1 - c, b], buf, buf, KI, ["terms"], add_ig(d, b, buf), rank=20 + b % 2)
    for b in range(4):
        for link, sg, buf in (("yu", 1, ryu), ("yd", -1, ryd)):
            dep, before = [f"c{sg}{b}"], None
            if (b < 2) == (link == "yu"):
                p.send(f"y2{b}", link, ig.at[yy(2), c, b], buf.at[0, b], buf.at[0, b], KI, [f"c2{b}"], rank=20 + b % 2)
                dep.append(f"y2{b}")
                before = add_ig(sg, b, buf.at[0, b])
            p.send(f"y1{link}{b}", link, ig.at[yy(sg), c, b], buf.at[1, b], buf.at[1, b], KI, dep, None, before, rank=20 + b % 2)

    def ig_sum(b):
        def fn():
            ig[y, c, b] += ryu[1, b] + ryd[1, b]

        return fn

    def ig_final(b):
        def fn():
            ig_out[:, b * 128 : (b + 1) * 128] = ig[y, c, b, 0:128] + rp[b]

        return fn

    for b in range(4):
        p.send(
            f"p{b}", "cross", ig.at[y, c, b, pl.ds(128, 128)], rp.at[b], rp.at[b], KI // 2,
            [f"y1yu{b}", f"y1yd{b}", f"c0{b}"], ig_final(b), ig_sum(b), rank=20,
        )

    zorder = (HZ, 3, -3, 2, -2, 1, -1, 0)

    def add_to(ref, buf):
        def fn():
            ref[...] += buf[...]

        return fn

    def add2(ref, b1, b2):
        def fn():
            ref[...] += b1[...] + b2[...]

        return fn

    def weight_reduce(q, rank):
        (a0, an), (b0, bn) = CHUNKS[q]
        A, B = pl.ds(a0, an), pl.ds(b0, bn)
        ready = [f"grad{q}"]
        gA = lambda d, a, m: g.at[zz(d), js[a], ms[m], :, A]
        gB = lambda d, a, m: g.at[zz(d), js[a], ms[m], :, B]
        for n, d in enumerate(zorder):
            for m in range(2):
                buf = rx.at[n, ms[m], :, B]
                p.send(f"rx{q}{m}{d}", "in", gB(d, 1, m), buf, buf, bn * KF, ready, add_to(gB(d, 0, m), buf), rank=rank)

        def ring(tag, ref, bufs, size, m, deps, rank):
            for s in range(HZ):
                for link, sg in (("zu", 1), ("zd", -1)):
                    if s == 0 and (m == 0) != (link == "zu"):
                        continue
                    d = sg * (HZ - s)
                    dep, before = list(deps(HZ if s == 0 else d)), None
                    if s > 1 or (s == 1 and (m == 0) == (link == "zu")):
                        dep.append(f"r{q}{tag}{m}{link}{s - 1}")
                        before = add_to(ref(d), bufs[link](s - 1))
                    p.send(f"r{q}{tag}{m}{link}{s}", link, ref(d), bufs[link](s), bufs[link](s), size, dep, None, before, rank=rank)
            return [f"r{q}{tag}{m}{link}{HZ - 1}" for link in ("zu", "zd")]

        for m in range(2):
            bufs = {
                "zu": lambda s, m=m: rbu.at[s, ms[m], :, B],
                "zd": lambda s, m=m: rbd.at[s, ms[m], :, B],
            }
            fin = ring("B", lambda d, m=m: gB(d, 0, m), bufs, bn * KF, m, lambda d, m=m: [f"rx{q}{m}{d}"], rank)
            p.step(f"finB{q}{m}", 0.05, add2(gB(0, 0, m), bufs["zu"](HZ - 1), bufs["zd"](HZ - 1)), fin + [f"rx{q}{m}0"])
        for m in range(2):
            for a in (1, 0):
                bufs = {
                    "zu": lambda s, m=m, a=a: rau.at[s, js[a], ms[m], :, A],
                    "zd": lambda s, m=m, a=a: rad.at[s, js[a], ms[m], :, A],
                }
                tag = "AO"[a]
                fin = ring(tag, lambda d, m=m, a=a: gA(d, a, m), bufs, an * KF, m, lambda d: ready, rank + 5)
                p.step(f"fin{tag}{q}{m}", 0.05, add2(gA(0, a, m), bufs["zu"](HZ - 1), bufs["zd"](HZ - 1)), fin)
            buf = rax.at[ms[m], :, A]
            p.send(f"rax{q}{m}", "in", gA(0, 1, m), buf, buf, an * KF, [f"finO{q}{m}"], rank=rank - 1)
            p.step(f"sumA{q}{m}", 0.05, add_to(gA(0, 0, m), buf), [f"rax{q}{m}", f"finA{q}{m}"])
        p.send(f"cB{q}", "cross", g.at[z, j, 1 - hf, :, B], rc.at[:, B], rc.at[:, B], bn * KF, [f"finB{q}1"], rank=rank)
        p.send(f"cA{q}", "cross", g.at[z, j, 1 - hf, :, A], rc.at[:, A], rc.at[:, A], an * KF, [f"sumA{q}1"], rank=rank)
        return [f"finB{q}0", f"sumA{q}0"], [f"cB{q}", f"cA{q}"]

    outs = [weight_reduce(0, 30), weight_reduce(1, 32)]

    def own_out():
        for cp in lm:
            cp.wait()
        for m, out in enumerate((gu_out, gd_out)):
            out[pl.ds(NF * hf, NF)] = 0.9 * mom[m, pl.ds(NF * hf, NF)] + (1.0 / 64.0) * g[z, j, hf, m]

    def other_out():
        for m, out in enumerate((gu_out, gd_out)):
            out[pl.ds(oh, NF)] = 0.9 * mom[m, pl.ds(oh, NF)] + (1.0 / 64.0) * rc[m]

    p.step("own_out", 0.1, own_out, outs[0][0] + outs[1][0])
    p.step("other_out", 0.1, other_out, outs[0][1] + outs[1][1])
    p.run()


def finish(ig, mu, md, ig_out, mu_out, md_out, sem):
    copies = [pltpu.make_async_copy(s, d, sem.at[n]) for n, (s, d) in enumerate(((ig, ig_out), (mu, mu_out), (md, md_out)))]
    for cp in copies:
        cp.start()
    for cp in copies:
        cp.wait()


def shards(inputs, cotangent, up_blocks, down_blocks, up_index, down_index, mom_up, mom_down):
    f, kb, r, b = up_blocks.shape
    tiles = lambda a: a.reshape(f, kb // 2, 2 * r, b)
    rows8 = lambda a: a.reshape(16, 8, 32, b).transpose(0, 2, 1, 3)
    vm = lambda *s: pltpu.VMEM(s, F32)
    hbm = pl.BlockSpec(memory_space=pl.ANY)
    vmem = pl.BlockSpec(memory_space=pltpu.VMEM)
    tile = (2, 8, 128)
    out_shape = (
        jax.ShapeDtypeStruct((128, 512), F32),
        jax.ShapeDtypeStruct((f, *tile), F32),
        jax.ShapeDtypeStruct((f, *tile), F32),
    )
    ig, gu, gd = pl.pallas_call(
        kernel,
        out_shape=tuple(vm(*o.shape) for o in out_shape),
        in_specs=[hbm] * 8,
        out_specs=(vmem, vmem, vmem),
        scratch_shapes=[
            vm(2, 16, 32, 8, 128),
            vm(16, 32, 8, 128),
            vm(16, 32, 8, 128),
            vm(NZ, 2, 2, 2, NF, *tile),
            vm(NZ, 2, 2, 2, NF, *tile),
            vm(NF, 256, 128),
            vm(NF, 256, 128),
            vm(4 * NF + 1, 256, 128),
            vm(NY, 2, 4, 256, 128),
            vm(NZ // 2, 2, 2, 2, NF, *tile),
            vm(NZ // 2, 2, 2, 2, NF, *tile),
            vm(NZ // 2, 2, 2, NF, *tile),
            vm(NZ // 2, 2, 2, NF, *tile),
            vm(NZ, 2, 2, NF, *tile),
            vm(2, 2, NF, *tile),
            vm(2, NF, *tile),
            vm(NY, 4, 256, 128),
            vm(2, 4, 256, 128),
            vm(2, 4, 256, 128),
            vm(4, 128, 128),
            pltpu.VMEM((NF, 512, 128), BF),
            pltpu.VMEM((NF, 512, 128), BF),
            pltpu.SMEM((NF, 32), jnp.int32),
            pltpu.SMEM((kb, f), jnp.int32),
            pltpu.SMEM((kb, f), jnp.int32),
            vm(2, f, *tile),
            pltpu.SemaphoreType.DMA((8,)),
            pltpu.SemaphoreType.DMA((NSEND,)),
            pltpu.SemaphoreType.DMA((NRECV,)),
        ],
        compiler_params=pltpu.CompilerParams(
            collective_id=0, has_side_effects=True, vmem_limit_bytes=60 * 1024 * 1024
        ),
    )(up_index.T, down_index.T, rows8(inputs), rows8(cotangent), tiles(up_blocks), tiles(down_blocks), tiles(mom_up), tiles(mom_down))
    ig, mu, md = pl.pallas_call(
        finish, out_shape=out_shape, in_specs=[vmem] * 3, out_specs=(hbm,) * 3, scratch_shapes=[pltpu.SemaphoreType.DMA((3,))]
    )(*(pltpu.with_memory_space_constraint(a, pltpu.VMEM) for a in (ig, gu, gd)))
    return ig, mu.reshape(mom_up.shape), md.reshape(mom_down.shape)


def solution(mesh):
    return jax.shard_map(
        shards,
        mesh=mesh,
        in_specs=(
            P("tok", None),
            P("tok", None),
            P("hid", None, "tok", None),
            P("hid", None, "tok", None),
            P("hid", None),
            P("hid", None),
            P("hid", None, "tok", None),
            P("hid", None, "tok", None),
        ),
        out_specs=(P("tok", "hid"), P("hid", None, "tok", None), P("hid", None, "tok", None)),
        check_vma=False,
    )
```
